32 devices in a mesh: lon: 8 (over z, x), lat: 4 (over y, core).
Axes of the slice: x: 2, y: 2, z: 4, core: 2. Of those that a mesh axis runs over, the one named last changes fastest.
Arguments:
- increment: bfloat16 [256, 512, 128], P('lon', 'lat'), may hold values from -6 to 6
- jacobian: bfloat16 [512, 128, 3072], P(('lon', 'lat')), may hold values from -0.0625 to 0.0625
- lat_weight: float32 [512, 8], P(('lon', 'lat')), may hold values from 0.2 to 2
- centre: int32 [512], P(('lon', 'lat')), may hold values from 0 to 31
- west: int32 [512], P(('lon', 'lat')), may hold values from 0 to 32
- east: int32 [512], P(('lon', 'lat')), may hold values from 0 to 32
- lat_offset: int32 [512], P(('lon', 'lat')), may hold values from 0 to 504
- lev_offset: int32 [512], P(('lon', 'lat')), may hold values from 0 to 96
Outputs:
- departures: float32 [512, 128], P(('lon', 'lat'))
The draws below stay inside these ranges and needn't reach their ends.
All inputs are finite; a program needn't handle non-finite values.
Results may differ from the reference program's by a relative error of at most 0.0029.
Values may be sent and summed in bfloat16 or wider, within the bound.
A program may use at most 128 MiB of HBM per device.

```python
import math
import jax
import jax.numpy as jnp
from jax import lax

LON_DEV = 32
SLOTS = 16
LEV = 128
NTAN = 128
BLAT = 8
BLEV = 32
LON = 256
LAT = 512
SCANS = 512
N_LON = 8
N_LAT = 4


def place_ends(entries, key, least, largest):
    dims = entries.shape
    spot = [jax.random.randint(jax.random.fold_in(key, axis), (), 0, dims[axis]) for axis in range(len(dims))]
    entries = entries.at[tuple(spot)].set(least)
    longest = dims.index(max(dims))
    spot[longest] = (spot[longest] + 1) % dims[longest]
    return entries.at[tuple(spot)].set(largest)


def level_of(own_key, dims, pieces, low, high):
    factor_of, own = 1.0, jax.random.fold_in(own_key, 6)
    for dim, shards_of in pieces:
        heights = jnp.exp(jax.random.uniform(jax.random.fold_in(own, dim), (shards_of,), jnp.float32, low / len(pieces), high / len(pieces)))
        factor_of = factor_of * jnp.repeat(heights, dims[dim] // shards_of).reshape([-1 if axis == dim else 1 for axis in range(len(dims))])
    return factor_of


def scatter_about(own_key, dims, deviation, bound, pieces=(), held_as=jnp.bfloat16):
    entries = deviation * jax.random.normal(own_key, dims, jnp.float32)
    if pieces:
        entries = entries * level_of(own_key, dims, pieces, -0.22, 0.18)
    return jnp.clip(entries, -bound, bound).astype(held_as)


def setup_inputs(seed: int = 0) -> dict:
    splits = jax.random.split(jax.random.key(seed), 9)
    return {
        "increment": scatter_about(splits[0], (LON, LAT, LEV), 1.0, 6.0, ((0, 8), (1, 4))),
        "jacobian": scatter_about(splits[1], (SCANS, NTAN, 3 * LON_DEV * BLEV), (BLAT * LON_DEV * BLEV) ** -0.5, 0.0625, ((0, 32),)),
        "lat_weight": jnp.clip(jnp.exp(math.log(2.0) - 2.3025851 * jax.random.uniform(splits[2], (SCANS, BLAT), jnp.float32) ** level_of(splits[2], (SCANS, BLAT), ((0, 32),), -0.2, 0.2)), 0.2, 2.0),
        "centre": place_ends(jax.random.randint(splits[3], (SCANS,), 0, LON_DEV), jax.random.fold_in(splits[3], 1), 0, LON_DEV - 1).astype(jnp.int32),
        "west": place_ends(jax.random.randint(splits[4], (SCANS,), 0, LON_DEV + 1), jax.random.fold_in(splits[4], 1), 0, LON_DEV).astype(jnp.int32),
        "east": place_ends(jax.random.randint(splits[5], (SCANS,), 0, LON_DEV + 1), jax.random.fold_in(splits[5], 1), 0, LON_DEV).astype(jnp.int32),
        "lat_offset": place_ends(jax.random.randint(splits[6], (SCANS,), 0, LAT - BLAT + 1), jax.random.fold_in(splits[6], 1), 0, LAT - BLAT).astype(jnp.int32),
        "lev_offset": place_ends(jax.random.randint(splits[7], (SCANS,), 0, LEV - BLEV + 1), jax.random.fold_in(splits[7], 1), 0, LEV - BLEV).astype(jnp.int32),
    }


def reference(increment, jacobian, lat_weight, centre, west, east, lat_offset, lev_offset):
    span = 3 * LON_DEV
    longitude = LON_DEV * N_LON

    def one_scan(item):
        index, kmat, weights, mid, left, right, lat_first, lev_first = item
        sector = index // (SLOTS * N_LAT)
        rows = jnp.arange(span, dtype=jnp.int32)
        columns = ((sector * LON_DEV - LON_DEV + rows) % longitude).astype(jnp.int32)
        window = jnp.take(increment, columns, axis=0)
        zero = jnp.zeros((), jnp.int32)
        box = lax.dynamic_slice(window, (zero, lat_first.astype(jnp.int32), lev_first.astype(jnp.int32)), (span, BLAT, BLEV))
        profile = jnp.einsum("rjk,j->rk", box.astype(jnp.float32), weights.astype(jnp.float32), precision=lax.Precision.HIGHEST)
        keep = (rows >= LON_DEV + mid - left) & (rows <= LON_DEV + mid + right)
        profile = jnp.where(keep[:, None], profile, jnp.zeros_like(profile)).astype(jnp.bfloat16)
        return jnp.dot(kmat, profile.reshape(-1), preferred_element_type=jnp.float32)

    indices = jnp.arange(SCANS, dtype=jnp.int32)
    return lax.map(one_scan, (indices, jacobian, lat_weight, centre, west, east, lat_offset, lev_offset))
```

```python
import functools

import jax
import jax.numpy as jnp
from jax import lax
from jax.experimental import pallas as pl
from jax.experimental.pallas import tpu as pltpu
from jax.sharding import PartitionSpec as P

BLAT = 8
BLEV = 32
HALO = 8
FIELDS = 16
CHUNKS = (1, 1, 1)
MESH = pl.DeviceIdType.MESH


def kernel(
    nlon, nlat, inc_ref, jac_ref, weight_hbm, centre_hbm, west_hbm, east_hbm, row_hbm, level_hbm,
    out_ref, weight_ref, centre_ref, west_ref, east_ref, row_ref, level_ref, small_sem,
    ext, halo, jbuf, info, passing, sel, pieces, recv,
    inc_sem, jac_sem, swap_send, swap_recv, halo_send, halo_recv,
    info_send, info_recv, pass_send, pass_recv, piece_send, piece_recv,
):
    lon = lax.axis_index("lon")
    lat = lax.axis_index("lat")
    width, rows, lev = inc_ref.shape
    slots, ntan = out_ref.shape
    group = lev // BLEV
    nq = width // group
    part = nq // 2
    half = width // 2
    listed = nlat * slots
    packed = lev // FIELDS
    pair = lat // 2
    side = lax.rem(lat, 2)
    npair = nlat // 2

    load = pltpu.make_async_copy(
        inc_ref.at[pl.ds(side * half, half)], ext.at[side], inc_sem
    )
    jload = pltpu.make_async_copy(jac_ref, jbuf, jac_sem)

    def sector(t):
        return lax.rem(lon + t - 1 + nlon, nlon)

    odd = lax.rem(lon, 2)
    opening = 1 - lax.div(lon + nlon - 1, nlon)
    closing = lax.div(lon + 1, nlon)
    order = (1, 2 - 2 * odd, 2 * odd)

    def others(t):
        own = isinstance(t, int) and t == 1
        return [lax.rem(lat + d, nlat) for d in range(1 if own else 0, nlat)]

    def every(chosen):
        return [(t, l) for t in chosen for l in others(t)]

    peers = []
    for t in (0, 2, 1):
        for d in range(nlat):
            if t != 1 or d:
                peers.append((t, lax.rem(lat + d, nlat)))

    middle_sector = (nlon - 1) // 2
    first_sector, last_sector = lon == 0, lon == nlon - 1
    is_middle = lon == middle_sector

    barrier = pltpu.get_barrier_semaphore()
    for t, l in peers:
        to = sector(t) if t != 2 else sector(2) + closing * middle_sector
        pl.semaphore_signal(barrier, inc=1, device_id=(to, l), device_id_type=MESH)

    @pl.when(is_middle)
    def _():
        pl.semaphore_signal(barrier, inc=1, device_id=(0, lat), device_id_type=MESH)

    small = [
        pltpu.make_async_copy(source, target, small_sem.at[i])
        for i, (source, target) in enumerate(
            [
                (weight_hbm, weight_ref), (row_hbm, row_ref), (level_hbm, level_ref),
                (centre_hbm, centre_ref), (west_hbm, west_ref), (east_hbm, east_ref),
            ]
        )
    ]
    for copy in small:
        copy.start()
    load.start()
    jload.start()

    eye = lax.broadcasted_iota(jnp.int32, (slots, slots), 0) == lax.broadcasted_iota(
        jnp.int32, (slots, slots), 1
    )

    def column(row):
        row = jnp.broadcast_to(row.astype(jnp.float32), (slots, slots))
        return jnp.sum(jnp.where(eye, row, 0.0), axis=1, keepdims=True)

    for copy in small:
        copy.wait()
    lane = lax.broadcasted_iota(jnp.int32, (slots, lev), 1)
    head = jnp.zeros((slots, lev), jnp.float32)
    for j in range(BLAT):
        head = jnp.where(lane == j, column(weight_ref[j : j + 1, :]), head)
    head = jnp.where(lane == BLAT, column(row_ref[...]), head)
    head = jnp.where(lane == BLAT + 1, column(level_ref[...]), head)
    place = lax.broadcasted_iota(jnp.int32, (slots, lev), 0)
    spread = jnp.take_along_axis(head, lax.rem(lane, FIELDS), axis=1)
    spread = jnp.where(lane // FIELDS == lax.rem(place, packed), spread, 0.0)
    info[1, lat] = jnp.concatenate(
        [
            jnp.sum(spread[r * packed : (r + 1) * packed], axis=0, keepdims=True)
            for r in range(slots // packed)
        ],
        axis=0,
    )
    middle = width + column(centre_ref[...])
    first = middle - column(west_ref[...])
    last = middle + column(east_ref[...])

    between = is_middle.astype(jnp.int32)
    pl.semaphore_wait(barrier, len(peers) - (nlat - 1) * opening + nlat * between)

    def info_copy(t, l):
        return pltpu.make_async_remote_copy(
            src_ref=info.at[1, lat], dst_ref=info.at[2 - t, lat],
            send_sem=info_send.at[t, l], recv_sem=info_recv.at[2 - t, lat],
            device_id=(sector(t), l), device_id_type=MESH,
        )

    def relay_in():
        return pltpu.make_async_remote_copy(
            src_ref=info.at[1, lat], dst_ref=passing,
            send_sem=pass_send.at[nlat], recv_sem=pass_recv,
            device_id=(middle_sector, lat), device_id_type=MESH,
        )

    def relay_out(l):
        return pltpu.make_async_remote_copy(
            src_ref=passing, dst_ref=info.at[2, lat],
            send_sem=pass_send.at[l], recv_sem=info_recv.at[2, lat],
            device_id=(nlon - 1, l), device_id_type=MESH,
        )

    @pl.when(first_sector)
    def _():
        relay_in().start()

    @pl.when(lon > 0)
    def _():
        for l in others(0):
            info_copy(0, l).start()

    for t, l in every((2, 1)):
        info_copy(t, l).start()
    swap = pltpu.make_async_remote_copy(
        src_ref=inc_ref.at[pl.ds((1 - side) * half, half)], dst_ref=ext.at[side],
        send_sem=swap_send, recv_sem=swap_recv,
        device_id=(lon, pair * 2 + 1 - side), device_id_type=MESH,
    )

    def halo_copy(other):
        return pltpu.make_async_remote_copy(
            src_ref=inc_ref.at[pl.ds(other * half, half), pl.ds(0, HALO), :], dst_ref=halo,
            send_sem=halo_send.at[other], recv_sem=halo_recv,
            device_id=(lon, lax.rem(pair + npair - 1, npair) * 2 + other), device_id_type=MESH,
        )

    @pl.when(side == 0)
    def _():
        halo_copy(0).start()
        halo_copy(1).start()

    swap.start()

    @pl.when(is_middle)
    def _():
        relay_in().wait_recv()
        for l in others(0):
            relay_out(l).start()


    def info_wait(t, l):
        pltpu.make_async_remote_copy(
            src_ref=info.at[1, lat], dst_ref=info.at[t, l],
            send_sem=info_send.at[t, l], recv_sem=info_recv.at[t, l],
            device_id=(sector(t), l), device_id_type=MESH,
        ).wait_recv()

    def slot(u, l, c, step):
        return recv.at[u, l // 2, pl.ds(lax.rem(l, 2) * part + c * step, step)]

    def piece_copy(t, l, c, step):
        return pltpu.make_async_remote_copy(
            src_ref=pieces.at[t, l, pl.ds(c * step, step)], dst_ref=slot(2 - t, lat, c, step),
            send_sem=piece_send.at[t, l, c], recv_sem=piece_recv.at[2 - t, lat, c],
            device_id=(sector(t), l), device_id_type=MESH,
        )

    def piece_wait(t, l, c, step):
        pltpu.make_async_remote_copy(
            src_ref=pieces.at[t, l, pl.ds(c * step, step)], dst_ref=slot(t, l, c, step),
            send_sem=piece_send.at[t, l, c], recv_sem=piece_recv.at[t, l, c],
            device_id=(sector(t), l), device_id_type=MESH,
        ).wait_recv()

    depth = 2 * rows + HALO
    wide = lax.broadcasted_iota(jnp.int32, (listed, lev), 1)
    unpack = lax.rem(
        lax.rem(lax.broadcasted_iota(jnp.int32, (listed, lev), 0), packed) * FIELDS + wide, lev
    )
    base = (pair * 2 * rows).astype(jnp.float32)

    ready = False
    for t, chunks in zip(order, CHUNKS):
        step = part // chunks
        for l in others(t):
            info_wait(t, l)
        table = jnp.concatenate(
            [
                jnp.broadcast_to(info[t, l, r : r + 1, :], (packed, lev))
                for l in range(nlat)
                for r in range(slots // packed)
            ],
            axis=0,
        )
        table = jnp.take_along_axis(table, unpack, axis=1)
        local = table[:, BLAT : BLAT + 1] - base
        mine = (local >= 0.0) & (local < float(2 * rows))
        start = jnp.broadcast_to(local, (listed, lev)).astype(jnp.int32)
        mine = jnp.broadcast_to(mine.astype(jnp.int32), (listed, lev)) > 0
        parts = []
        for begin in range(0, depth, lev):
            offset = wide + begin - start
            good = mine & (offset >= 0) & (offset < BLAT)
            picked = jnp.take_along_axis(table, jnp.clip(offset, 0, lev - 1), axis=1)
            parts.append(jnp.where(good, picked, 0.0))
        whole = jnp.concatenate(parts, axis=1)[:, :depth]
        high = whole.astype(jnp.bfloat16)
        low = (whole - high.astype(jnp.float32)).astype(jnp.bfloat16)
        sel[0:listed, :] = high
        sel[listed : 2 * listed, :] = low
        where = jnp.broadcast_to(table[:, BLAT + 1 : BLAT + 2], (listed, lev)).astype(
            jnp.int32
        ) + lax.rem(wide, BLEV)
        if not ready:
            load.wait()
            swap.wait_recv()
            halo_copy(0).wait_recv()
            ready = True

        for q in range(part):
            right = jnp.concatenate(
                [
                    jnp.concatenate(
                        [ext[0, q * group + g], ext[1, q * group + g], halo[q * group + g]], axis=0
                    )
                    for g in range(group)
                ],
                axis=1,
            )
            lifted = jnp.dot(sel[...], right, preferred_element_type=jnp.float32)
            lifted = lifted[:listed] + lifted[listed:]
            total = jnp.zeros((listed, lev), jnp.float32)
            for g in range(group):
                moved = jnp.take_along_axis(lifted[:, g * lev : (g + 1) * lev], where, axis=1)
                inside = (wide >= g * BLEV) & (wide < (g + 1) * BLEV)
                total = jnp.where(inside, moved, total)
            total = total.astype(jnp.bfloat16)
            for l in range(nlat):
                pieces[t, l, q] = total[l * slots : (l + 1) * slots]
            if (q + 1) % step == 0:
                for l in others(t):
                    piece_copy(t, l, q // step, step).start()

    keep = pltpu.make_async_copy(
        pieces.at[1, lat], recv.at[1, pair, pl.ds(side * part, part)], inc_sem
    )
    keep.start()
    jload.wait()
    keep.wait()
    span = width * BLEV
    level_row = (lax.broadcasted_iota(jnp.int32, (slots, lev), 1) // BLEV).astype(jnp.float32)
    which = lax.broadcasted_iota(jnp.int32, (slots, ntan), 0)
    answer = jnp.zeros((slots, ntan), jnp.float32)
    for t, chunks in zip(order, CHUNKS):
        step = part // chunks
        across = step * lev
        for c in range(chunks):
            for l in others(t):
                piece_wait(t, l, c, step)
            flat = []
            for h in range(2):
                for q in range(c * step, (c + 1) * step):
                    total = recv[t, 0, h * part + q].astype(jnp.float32)
                    for p in range(1, npair):
                        total = total + recv[t, p, h * part + q].astype(jnp.float32)
                    begin = t * width + (h * part + q) * group
                    at = level_row + jnp.asarray(begin, jnp.int32).astype(jnp.float32)
                    flat.append(jnp.where((at >= first) & (at <= last), total, 0.0))
            flat = jnp.concatenate(flat, axis=1).astype(jnp.bfloat16)

            for i in range(slots // 2):
                block = []
                for h in range(2):
                    begin = t * span + h * (span // 2) + c * across
                    if not isinstance(begin, int):
                        begin = pl.multiple_of(begin, lev)
                    block.append(
                        jbuf[2 * i : 2 * i + 2, :, pl.ds(begin, across)].reshape(2 * ntan, across)
                    )
                both = lax.dot_general(
                    flat, jnp.concatenate(block, axis=1), (((1,), (1,)), ((), ())),
                    preferred_element_type=jnp.float32,
                )
                answer = answer + jnp.where(which == 2 * i, both[:, :ntan], 0.0)
                answer = answer + jnp.where(which == 2 * i + 1, both[:, ntan:], 0.0)
    out_ref[...] = answer

    swap.wait_send()

    @pl.when(side == 0)
    def _():
        halo_copy(0).wait_send()
        halo_copy(1).wait_send()

    @pl.when(first_sector)
    def _():
        relay_in().wait_send()

    @pl.when(lon > 0)
    def _():
        for l in others(0):
            info_copy(0, l).wait_send()

    @pl.when(is_middle)
    def _():
        for l in others(0):
            relay_out(l).wait_send()

    for t, l in every((2, 1)):
        info_copy(t, l).wait_send()
    for t, chunks in zip(order, CHUNKS):
        for l in others(t):
            for c in range(chunks):
                piece_copy(t, l, c, part // chunks).wait_send()


def local(nlon, nlat, increment, jacobian, lat_weight, centre, west, east, lat_offset, lev_offset):
    width, rows, lev = increment.shape
    slots, ntan, span = jacobian.shape
    nq = width * BLEV // lev
    vmem = pl.BlockSpec(memory_space=pltpu.VMEM)
    hbm = pl.BlockSpec(memory_space=pltpu.HBM)
    dma = pltpu.SemaphoreType.DMA
    ints = [v.reshape(1, slots) for v in (centre, west, east, lat_offset, lev_offset)]
    return pl.pallas_call(
        functools.partial(kernel, nlon, nlat),
        out_shape=pltpu.VMEM((slots, ntan), jnp.float32),
        in_specs=[hbm] * 8,
        out_specs=vmem,
        scratch_shapes=[
            pltpu.VMEM((BLAT, slots), jnp.float32),
            *[pltpu.VMEM((1, slots), jnp.int32)] * 5,
            dma((6,)),
            pltpu.VMEM((2, width // 2, rows, lev), jnp.bfloat16),
            pltpu.VMEM((width // 2, HALO, lev), jnp.bfloat16),
            pltpu.VMEM((slots, ntan, span), jnp.bfloat16),
            pltpu.VMEM((3, nlat, slots * FIELDS // lev, lev), jnp.float32),
            pltpu.VMEM((slots * FIELDS // lev, lev), jnp.float32),
            pltpu.VMEM((2 * nlat * slots, 2 * rows + HALO), jnp.bfloat16),
            pltpu.VMEM((3, nlat, nq // 2, slots, lev), jnp.bfloat16),
            pltpu.VMEM((3, nlat // 2, nq, slots, lev), jnp.bfloat16),
            dma, dma, dma, dma, dma((2,)), dma,
            dma((3, nlat)), dma((3, nlat)), dma((nlat + 1,)), dma, dma((3, nlat, max(CHUNKS))), dma((3, nlat, max(CHUNKS))),
        ],
        compiler_params=pltpu.CompilerParams(
            collective_id=0, has_side_effects=True, vmem_limit_bytes=56 << 20
        ),
    )(increment, jacobian, lat_weight.T, *ints)


def solution(mesh):
    return jax.shard_map(
        functools.partial(local, mesh.shape["lon"], mesh.shape["lat"]),
        mesh=mesh,
        in_specs=(
            P("lon", "lat", None),
            P(("lon", "lat"), None, None),
            P(("lon", "lat"), None),
            P(("lon", "lat")),
            P(("lon", "lat")),
            P(("lon", "lat")),
            P(("lon", "lat")),
            P(("lon", "lat")),
        ),
        out_specs=P(("lon", "lat"), None),
        check_vma=False,
    )
```

```python
import functools

import jax
import jax.numpy as jnp
from jax import lax
from jax.experimental import pallas as pl
from jax.experimental.pallas import tpu as pltpu
from jax.sharding import PartitionSpec as P

BLAT = 8
BLEV = 32
HALO = 8
FIELDS = 16
CHUNKS = (1, 1, 1)
MESH = pl.DeviceIdType.MESH


def kernel(
    nlon, nlat, inc_ref, jac_ref, weight_hbm, centre_hbm, west_hbm, east_hbm, row_hbm, level_hbm,
    out_ref, weight_ref, centre_ref, west_ref, east_ref, row_ref, level_ref, small_sem,
    ext, halo, jbuf, turned, info, sel, pieces, recv,
    inc_sem, jac_sem, swap_send, swap_recv, halo_send, halo_recv,
    info_send, info_recv, pass_send, pass_recv, piece_send, piece_recv,
):
    lon = lax.axis_index("lon")
    lat = lax.axis_index("lat")
    width, rows, lev = inc_ref.shape
    slots, ntan = out_ref.shape
    group = lev // BLEV
    nq = width // group
    part = nq // 2
    half = width // 2
    listed = nlat * slots
    packed = lev // FIELDS
    pair = lat // 2
    side = lax.rem(lat, 2)
    npair = nlat // 2

    load = pltpu.make_async_copy(
        inc_ref.at[pl.ds(side * half, half)], ext.at[side], inc_sem
    )
    jload = pltpu.make_async_copy(jac_ref, jbuf, jac_sem)

    def sector(t):
        return lax.rem(lon + t - 1 + nlon, nlon)

    first_sector, relay_sector, last_sector = lon == 0, lon == 1, lon == nlon - 1
    odd = lax.rem(lon, 2)
    opening = first_sector.astype(jnp.int32)
    closing = last_sector.astype(jnp.int32)
    ahead = odd - closing
    later = odd + (lon == nlon - 2).astype(jnp.int32)
    relaying = relay_sector.astype(jnp.int32)
    serve = (1 - relaying, 2 - 2 * ahead + relaying, 2 * ahead)
    collect = (1, 2 - 2 * later, 2 * later)

    def others(t):
        own = isinstance(t, int) and t == 1
        return [lax.rem(lat + d, nlat) for d in range(1 if own else 0, nlat)]

    def every(chosen):
        return [(t, l) for t in chosen for l in others(t)]

    peers = []
    for t in (0, 2, 1):
        for d in range(nlat):
            if t != 1 or d:
                peers.append((t, lax.rem(lat + d, nlat)))

    barrier = pltpu.get_barrier_semaphore()

    def greet(t, l):
        pl.semaphore_signal(barrier, inc=1, device_id=(sector(t), l), device_id_type=MESH)

    @pl.when(last_sector)
    def _():
        pl.semaphore_signal(barrier, inc=1, device_id=(1, lat), device_id_type=MESH)

    @pl.when(lon < nlon - 1)
    def _():
        for l in others(2):
            greet(2, l)

    for t, l in every((0, 1)):
        greet(t, l)
    small = [
        pltpu.make_async_copy(source, target, small_sem.at[i])
        for i, (source, target) in enumerate(
            [
                (weight_hbm, weight_ref), (row_hbm, row_ref), (level_hbm, level_ref),
                (centre_hbm, centre_ref), (west_hbm, west_ref), (east_hbm, east_ref),
            ]
        )
    ]
    for copy in small:
        copy.start()
    load.start()
    jload.start()

    eye = lax.broadcasted_iota(jnp.int32, (slots, slots), 0) == lax.broadcasted_iota(
        jnp.int32, (slots, slots), 1
    )

    def column(row):
        row = jnp.broadcast_to(row.astype(jnp.float32), (slots, slots))
        return jnp.sum(jnp.where(eye, row, 0.0), axis=1, keepdims=True)

    for copy in small:
        copy.wait()
    lane = lax.broadcasted_iota(jnp.int32, (slots, lev), 1)
    head = jnp.zeros((slots, lev), jnp.float32)
    for j in range(BLAT):
        head = jnp.where(lane == j, column(weight_ref[j : j + 1, :]), head)
    head = jnp.where(lane == BLAT, column(row_ref[...]), head)
    head = jnp.where(lane == BLAT + 1, column(level_ref[...]), head)
    place = lax.broadcasted_iota(jnp.int32, (slots, lev), 0)
    spread = jnp.take_along_axis(head, lax.rem(lane, FIELDS), axis=1)
    spread = jnp.where(lane // FIELDS == lax.rem(place, packed), spread, 0.0)
    info[1, lat] = jnp.concatenate(
        [
            jnp.sum(spread[r * packed : (r + 1) * packed], axis=0, keepdims=True)
            for r in range(slots // packed)
        ],
        axis=0,
    )
    middle = width + column(centre_ref[...])
    first = middle - column(west_ref[...])
    last = middle + column(east_ref[...])

    pl.semaphore_wait(
        barrier, len(peers) - nlat * opening + relay_sector.astype(jnp.int32)
    )

    def info_copy(t, l):
        return pltpu.make_async_remote_copy(
            src_ref=info.at[1, lat], dst_ref=info.at[2 - t, lat],
            send_sem=info_send.at[t, l], recv_sem=info_recv.at[2 - t, lat],
            device_id=(sector(t), l), device_id_type=MESH,
        )

    relay = pltpu.make_async_remote_copy(
        src_ref=info.at[0], dst_ref=info.at[2], send_sem=pass_send, recv_sem=pass_recv,
        device_id=(nlon - 1, lat), device_id_type=MESH,
    )

    @pl.when(lon > 0)
    def _():
        for l in others(0):
            info_copy(0, l).start()

    for t, l in every((2, 1)):
        info_copy(t, l).start()
    swap = pltpu.make_async_remote_copy(
        src_ref=inc_ref.at[pl.ds((1 - side) * half, half)], dst_ref=ext.at[side],
        send_sem=swap_send, recv_sem=swap_recv,
        device_id=(lon, pair * 2 + 1 - side), device_id_type=MESH,
    )

    def halo_copy(other):
        return pltpu.make_async_remote_copy(
            src_ref=inc_ref.at[pl.ds(other * half, half), pl.ds(0, HALO), :], dst_ref=halo,
            send_sem=halo_send.at[other], recv_sem=halo_recv,
            device_id=(lon, lax.rem(pair + npair - 1, npair) * 2 + other), device_id_type=MESH,
        )

    @pl.when(side == 0)
    def _():
        halo_copy(0).start()
        halo_copy(1).start()

    swap.start()

    def info_wait(t, l):
        pltpu.make_async_remote_copy(
            src_ref=info.at[1, lat], dst_ref=info.at[t, l],
            send_sem=info_send.at[t, l], recv_sem=info_recv.at[t, l],
            device_id=(sector(t), l), device_id_type=MESH,
        ).wait_recv()

    @pl.when(relay_sector)
    def _():
        for l in others(0):
            info_wait(0, l)
        relay.start()

    def slot(u, l, c, step):
        return recv.at[u, l // 2, pl.ds(lax.rem(l, 2) * part + c * step, step)]

    def piece_copy(t, l, c, step):
        return pltpu.make_async_remote_copy(
            src_ref=pieces.at[t, l, pl.ds(c * step, step)], dst_ref=slot(2 - t, lat, c, step),
            send_sem=piece_send.at[t, l, c], recv_sem=piece_recv.at[2 - t, lat, c],
            device_id=(sector(t), l), device_id_type=MESH,
        )

    def piece_wait(t, l, c, step):
        pltpu.make_async_remote_copy(
            src_ref=pieces.at[t, l, pl.ds(c * step, step)], dst_ref=slot(t, l, c, step),
            send_sem=piece_send.at[t, l, c], recv_sem=piece_recv.at[t, l, c],
            device_id=(sector(t), l), device_id_type=MESH,
        ).wait_recv()

    depth = 2 * rows + HALO
    wide = lax.broadcasted_iota(jnp.int32, (listed, lev), 1)
    unpack = lax.rem(
        lax.rem(lax.broadcasted_iota(jnp.int32, (listed, lev), 0), packed) * FIELDS + wide, lev
    )
    base = (pair * 2 * rows).astype(jnp.float32)

    ready = False
    for place_of, (t, chunks) in enumerate(zip(serve, CHUNKS)):
        step = part // chunks
        if place_of == 0:
            @pl.when(lon != 1)
            def _():
                for l in others(1):
                    info_wait(1, l)
        elif place_of == 1:
            @pl.when(last_sector)
            def _():
                relay.wait_recv()

            @pl.when(relay_sector)
            def _():
                for l in others(1):
                    info_wait(1, l)

            @pl.when((lon > 1) & (lon < nlon - 1) | first_sector)
            def _():
                for l in others(t):
                    info_wait(t, l)
        else:
            for l in others(t):
                info_wait(t, l)
        table = jnp.concatenate(
            [
                jnp.broadcast_to(info[t, l, r : r + 1, :], (packed, lev))
                for l in range(nlat)
                for r in range(slots // packed)
            ],
            axis=0,
        )
        table = jnp.take_along_axis(table, unpack, axis=1)
        local = table[:, BLAT : BLAT + 1] - base
        mine = (local >= 0.0) & (local < float(2 * rows))
        start = jnp.broadcast_to(local, (listed, lev)).astype(jnp.int32)
        mine = jnp.broadcast_to(mine.astype(jnp.int32), (listed, lev)) > 0
        parts = []
        for begin in range(0, depth, lev):
            offset = wide + begin - start
            good = mine & (offset >= 0) & (offset < BLAT)
            picked = jnp.take_along_axis(table, jnp.clip(offset, 0, lev - 1), axis=1)
            parts.append(jnp.where(good, picked, 0.0))
        whole = jnp.concatenate(parts, axis=1)[:, :depth]
        high = whole.astype(jnp.bfloat16)
        low = (whole - high.astype(jnp.float32)).astype(jnp.bfloat16)
        sel[0:listed, :] = high
        sel[listed : 2 * listed, :] = low
        where = jnp.broadcast_to(table[:, BLAT + 1 : BLAT + 2], (listed, lev)).astype(
            jnp.int32
        ) + lax.rem(wide, BLEV)
        if not ready:
            load.wait()
            swap.wait_recv()
            halo_copy(0).wait_recv()
            ready = True

        for q in range(part):
            right = jnp.concatenate(
                [
                    jnp.concatenate(
                        [ext[0, q * group + g], ext[1, q * group + g], halo[q * group + g]], axis=0
                    )
                    for g in range(group)
                ],
                axis=1,
            )
            lifted = jnp.dot(sel[...], right, preferred_element_type=jnp.float32)
            lifted = lifted[:listed] + lifted[listed:]
            total = jnp.zeros((listed, lev), jnp.float32)
            for g in range(group):
                moved = jnp.take_along_axis(lifted[:, g * lev : (g + 1) * lev], where, axis=1)
                inside = (wide >= g * BLEV) & (wide < (g + 1) * BLEV)
                total = jnp.where(inside, moved, total)
            total = total.astype(jnp.bfloat16)
            for l in range(nlat):
                pieces[t, l, q] = total[l * slots : (l + 1) * slots]
            if (q + 1) % step == 0:
                for l in range(nlat):
                    if place_of == 2:
                        piece_copy(t, l, q // step, step).start()
                    else:
                        @pl.when((t != 1) | (lat != l))
                        def _():
                            piece_copy(t, l, q // step, step).start()

    keep = pltpu.make_async_copy(
        pieces.at[1, lat], recv.at[1, pair, pl.ds(side * part, part)], inc_sem
    )
    keep.start()
    jload.wait()
    keep.wait()
    span = width * BLEV
    level_row = (lax.broadcasted_iota(jnp.int32, (slots, lev), 1) // BLEV).astype(jnp.float32)
    which = lax.broadcasted_iota(jnp.int32, (slots, ntan), 0)
    answer = jnp.zeros((slots, ntan), jnp.float32)
    def begin_of(t):
        return t * span if isinstance(t, int) else pl.multiple_of(t * span, lev)

    def turn(k):
        for i in range(slots):
            turned[k, i // 2, :, pl.ds((i % 2) * ntan, ntan)] = jbuf[
                i, :, pl.ds(begin_of(collect[k + 1]), span)
            ].T

    def profile(t, low, high):
        flat = []
        for q in range(low, high):
            total = recv[t, 0, q].astype(jnp.float32)
            for p in range(1, npair):
                total = total + recv[t, p, q].astype(jnp.float32)
            at = level_row + jnp.asarray(t * width + q * group, jnp.int32).astype(jnp.float32)
            flat.append(jnp.where((at >= first) & (at <= last), total, 0.0))
        return jnp.concatenate(flat, axis=1).astype(jnp.bfloat16)

    for k, t in enumerate(collect):
        if k == 0:
            turn(1)
        if k == 2:
            for h in (1, 0):
                for l in range(h, nlat, 2):
                    piece_wait(t, l, 0, part)
                flat = profile(t, h * part, (h + 1) * part)
                for i in range(slots // 2):
                    both = jnp.dot(
                        flat, turned[1, i, h * (span // 2) : (h + 1) * (span // 2)],
                        preferred_element_type=jnp.float32,
                    )
                    answer = answer + jnp.where(which == 2 * i, both[:, :ntan], 0.0)
                    answer = answer + jnp.where(which == 2 * i + 1, both[:, ntan:], 0.0)
            break
        for l in others(t):
            piece_wait(t, l, 0, part)
        flat = profile(t, 0, nq)
        for i in range(slots // 2):
            if k == 0:
                block = jbuf[2 * i : 2 * i + 2, :, pl.ds(begin_of(t), span)].reshape(2 * ntan, span)
                both = lax.dot_general(
                    flat, block, (((1,), (1,)), ((), ())), preferred_element_type=jnp.float32
                )
            else:
                both = jnp.dot(flat, turned[k - 1, i], preferred_element_type=jnp.float32)
            answer = answer + jnp.where(which == 2 * i, both[:, :ntan], 0.0)
            answer = answer + jnp.where(which == 2 * i + 1, both[:, ntan:], 0.0)
        if k == 0:
            turn(0)
    out_ref[...] = answer

    swap.wait_send()

    @pl.when(side == 0)
    def _():
        halo_copy(0).wait_send()
        halo_copy(1).wait_send()

    @pl.when(lon > 0)
    def _():
        for l in others(0):
            info_copy(0, l).wait_send()

    @pl.when(relay_sector)
    def _():
        relay.wait_send()

    for t, l in every((2, 1)):
        info_copy(t, l).wait_send()
    for t, l in peers:
        piece_copy(t, l, 0, part).wait_send()


def local(nlon, nlat, increment, jacobian, lat_weight, centre, west, east, lat_offset, lev_offset):
    width, rows, lev = increment.shape
    slots, ntan, span = jacobian.shape
    nq = width * BLEV // lev
    vmem = pl.BlockSpec(memory_space=pltpu.VMEM)
    hbm = pl.BlockSpec(memory_space=pltpu.HBM)
    dma = pltpu.SemaphoreType.DMA
    ints = [v.reshape(1, slots) for v in (centre, west, east, lat_offset, lev_offset)]
    return pl.pallas_call(
        functools.partial(kernel, nlon, nlat),
        out_shape=pltpu.VMEM((slots, ntan), jnp.float32),
        in_specs=[hbm] * 8,
        out_specs=vmem,
        scratch_shapes=[
            pltpu.VMEM((BLAT, slots), jnp.float32),
            *[pltpu.VMEM((1, slots), jnp.int32)] * 5,
            dma((6,)),
            pltpu.VMEM((2, width // 2, rows, lev), jnp.bfloat16),
            pltpu.VMEM((width // 2, HALO, lev), jnp.bfloat16),
            pltpu.VMEM((slots, ntan, span), jnp.bfloat16),
            pltpu.VMEM((2, slots // 2, width * BLEV, 2 * ntan), jnp.bfloat16),
            pltpu.VMEM((3, nlat, slots * FIELDS // lev, lev), jnp.float32),
            pltpu.VMEM((2 * nlat * slots, 2 * rows + HALO), jnp.bfloat16),
            pltpu.VMEM((3, nlat, nq // 2, slots, lev), jnp.bfloat16),
            pltpu.VMEM((3, nlat // 2, nq, slots, lev), jnp.bfloat16),
            dma, dma, dma, dma, dma((2,)), dma,
            dma((3, nlat)), dma((3, nlat)), dma, dma, dma((3, nlat, max(CHUNKS))), dma((3, nlat, max(CHUNKS))),
        ],
        compiler_params=pltpu.CompilerParams(
            collective_id=0, has_side_effects=True, vmem_limit_bytes=56 << 20
        ),
    )(increment, jacobian, lat_weight.T, *ints)


def solution(mesh):
    return jax.shard_map(
        functools.partial(local, mesh.shape["lon"], mesh.shape["lat"]),
        mesh=mesh,
        in_specs=(
            P("lon", "lat", None),
            P(("lon", "lat"), None, None),
            P(("lon", "lat"), None),
            P(("lon", "lat")),
            P(("lon", "lat")),
            P(("lon", "lat")),
            P(("lon", "lat")),
            P(("lon", "lat")),
        ),
        out_specs=P(("lon", "lat"), None),
        check_vma=False,
    )
```

```python
import functools

import jax
import jax.numpy as jnp
from jax import lax
from jax.experimental import pallas as pl
from jax.experimental.pallas import tpu as pltpu
from jax.sharding import PartitionSpec as P

BLAT = 8
BLEV = 32
HALO = 8
FIELDS = 16
CHUNKS = 1
MESH = pl.DeviceIdType.MESH


def kernel(
    nlon, nlat, inc_ref, jac_ref, weight_hbm, centre_hbm, west_hbm, east_hbm, row_hbm, level_hbm,
    out_ref, weight_ref, centre_ref, west_ref, east_ref, row_ref, level_ref, small_sem,
    ext, halo, jbuf, turned, info, sel, pieces, recv,
    inc_sem, jac_sem, swap_send, swap_recv, halo_send, halo_recv,
    info_send, info_recv, pass_send, pass_recv, piece_send, piece_recv,
):
    lon = lax.axis_index("lon")
    lat = lax.axis_index("lat")
    width, rows, lev = inc_ref.shape
    slots, ntan = out_ref.shape
    group = lev // BLEV
    nq = width // group
    part = nq // 2
    half = width // 2
    listed = nlat * slots
    packed = lev // FIELDS
    pair = lat // 2
    side = lax.rem(lat, 2)
    npair = nlat // 2

    load = pltpu.make_async_copy(
        inc_ref.at[pl.ds(side * half, half)], ext.at[side], inc_sem
    )
    jload = pltpu.make_async_copy(jac_ref, jbuf, jac_sem)

    def sector(t):
        return lax.rem(lon + t - 1 + nlon, nlon)

    first_sector, relay_sector, last_sector = lon == 0, lon == 1, lon == nlon - 1
    odd = lax.rem(lon, 2)
    opening = first_sector.astype(jnp.int32)
    closing = last_sector.astype(jnp.int32)
    ahead = odd - closing
    later = odd + (lon == nlon - 2).astype(jnp.int32)
    relaying = relay_sector.astype(jnp.int32)
    serve = (1 - relaying, 2 - 2 * ahead + relaying, 2 * ahead)
    collect = (1, 2 - 2 * later, 2 * later)

    def others(t):
        own = isinstance(t, int) and t == 1
        return [lax.rem(lat + d, nlat) for d in range(1 if own else 0, nlat)]

    def every(chosen):
        return [(t, l) for t in chosen for l in others(t)]

    peers = []
    for t in (0, 2, 1):
        for d in range(nlat):
            if t != 1 or d:
                peers.append((t, lax.rem(lat + d, nlat)))

    barrier = pltpu.get_barrier_semaphore()

    def greet(t, l):
        pl.semaphore_signal(barrier, inc=1, device_id=(sector(t), l), device_id_type=MESH)

    @pl.when(last_sector)
    def _():
        pl.semaphore_signal(
            barrier, inc=1, device_id=(1, pair * 2 + 1), device_id_type=MESH
        )

    @pl.when(lon < nlon - 1)
    def _():
        for l in others(2):
            greet(2, l)

    for t, l in every((0, 1)):
        greet(t, l)
    small = [
        pltpu.make_async_copy(source, target, small_sem.at[i])
        for i, (source, target) in enumerate(
            [
                (weight_hbm, weight_ref), (row_hbm, row_ref), (level_hbm, level_ref),
                (centre_hbm, centre_ref), (west_hbm, west_ref), (east_hbm, east_ref),
            ]
        )
    ]
    for copy in small:
        copy.start()
    load.start()
    jload.start()

    eye = lax.broadcasted_iota(jnp.int32, (slots, slots), 0) == lax.broadcasted_iota(
        jnp.int32, (slots, slots), 1
    )

    def column(row):
        row = jnp.broadcast_to(row.astype(jnp.float32), (slots, slots))
        return jnp.sum(jnp.where(eye, row, 0.0), axis=1, keepdims=True)

    for copy in small:
        copy.wait()
    lane = lax.broadcasted_iota(jnp.int32, (slots, lev), 1)
    head = jnp.zeros((slots, lev), jnp.float32)
    for j in range(BLAT):
        head = jnp.where(lane == j, column(weight_ref[j : j + 1, :]), head)
    head = jnp.where(lane == BLAT, column(row_ref[...]), head)
    head = jnp.where(lane == BLAT + 1, column(level_ref[...]), head)
    place = lax.broadcasted_iota(jnp.int32, (slots, lev), 0)
    spread = jnp.take_along_axis(head, lax.rem(lane, FIELDS), axis=1)
    spread = jnp.where(lane // FIELDS == lax.rem(place, packed), spread, 0.0)
    info[1, lat] = jnp.concatenate(
        [
            jnp.sum(spread[r * packed : (r + 1) * packed], axis=0, keepdims=True)
            for r in range(slots // packed)
        ],
        axis=0,
    )
    middle = width + column(centre_ref[...])
    first = middle - column(west_ref[...])
    last = middle + column(east_ref[...])

    pl.semaphore_wait(
        barrier, len(peers) - nlat * opening + 2 * relaying * side
    )

    def info_copy(t, l):
        return pltpu.make_async_remote_copy(
            src_ref=info.at[1, lat], dst_ref=info.at[2 - t, lat],
            send_sem=info_send.at[t, l], recv_sem=info_recv.at[2 - t, lat],
            device_id=(sector(t), l), device_id_type=MESH,
        )

    def relay(other):
        return pltpu.make_async_remote_copy(
            src_ref=info.at[0], dst_ref=info.at[2],
            send_sem=pass_send.at[other], recv_sem=pass_recv,
            device_id=(nlon - 1, pair * 2 + other), device_id_type=MESH,
        )

    @pl.when(lon > 0)
    def _():
        for l in others(0):
            info_copy(0, l).start()

    for t, l in every((2, 1)):
        info_copy(t, l).start()
    swap = pltpu.make_async_remote_copy(
        src_ref=inc_ref.at[pl.ds((1 - side) * half, half)], dst_ref=ext.at[side],
        send_sem=swap_send, recv_sem=swap_recv,
        device_id=(lon, pair * 2 + 1 - side), device_id_type=MESH,
    )

    def halo_copy(other):
        return pltpu.make_async_remote_copy(
            src_ref=inc_ref.at[pl.ds(other * half, half), pl.ds(0, HALO), :], dst_ref=halo,
            send_sem=halo_send.at[other], recv_sem=halo_recv,
            device_id=(lon, lax.rem(pair + npair - 1, npair) * 2 + other), device_id_type=MESH,
        )

    @pl.when(side == 0)
    def _():
        halo_copy(0).start()
        halo_copy(1).start()

    swap.start()

    def info_wait(t, l):
        pltpu.make_async_remote_copy(
            src_ref=info.at[1, lat], dst_ref=info.at[t, l],
            send_sem=info_send.at[t, l], recv_sem=info_recv.at[t, l],
            device_id=(sector(t), l), device_id_type=MESH,
        ).wait_recv()

    @pl.when(relay_sector & (side == 1))
    def _():
        for l in others(0):
            info_wait(0, l)
        relay(0).start()
        relay(1).start()

    def slot(u, l, c, step):
        return recv.at[u, l // 2, pl.ds(lax.rem(l, 2) * part + c * step, step)]

    def piece_copy(t, l, c, step):
        return pltpu.make_async_remote_copy(
            src_ref=pieces.at[t, l, pl.ds(c * step, step)], dst_ref=slot(2 - t, lat, c, step),
            send_sem=piece_send.at[t, l], recv_sem=piece_recv.at[2 - t, lat],
            device_id=(sector(t), l), device_id_type=MESH,
        )

    def piece_wait(t, l, c, step):
        pltpu.make_async_remote_copy(
            src_ref=pieces.at[t, l, pl.ds(c * step, step)], dst_ref=slot(t, l, c, step),
            send_sem=piece_send.at[t, l], recv_sem=piece_recv.at[t, l],
            device_id=(sector(t), l), device_id_type=MESH,
        ).wait_recv()

    depth = 2 * rows + HALO
    wide = lax.broadcasted_iota(jnp.int32, (listed, lev), 1)
    unpack = lax.rem(
        lax.rem(lax.broadcasted_iota(jnp.int32, (listed, lev), 0), packed) * FIELDS + wide, lev
    )
    base = (pair * 2 * rows).astype(jnp.float32)

    ready = False
    step = part // CHUNKS
    for place_of, t in enumerate(serve):
        if place_of == 0:
            @pl.when(lon != 1)
            def _():
                for l in others(1):
                    info_wait(1, l)

            @pl.when(relay_sector & (side == 0))
            def _():
                for l in others(0):
                    info_wait(0, l)
        elif place_of == 1:
            @pl.when(last_sector)
            def _():
                relay(0).wait_recv()

            @pl.when(relay_sector)
            def _():
                for l in others(1):
                    info_wait(1, l)

            @pl.when((lon > 1) & (lon < nlon - 1) | first_sector)
            def _():
                for l in others(t):
                    info_wait(t, l)
        else:
            for l in others(t):
                info_wait(t, l)
        table = jnp.concatenate(
            [
                jnp.broadcast_to(info[t, l, r : r + 1, :], (packed, lev))
                for l in range(nlat)
                for r in range(slots // packed)
            ],
            axis=0,
        )
        table = jnp.take_along_axis(table, unpack, axis=1)
        local = table[:, BLAT : BLAT + 1] - base
        mine = (local >= 0.0) & (local < float(2 * rows))
        start = jnp.broadcast_to(local, (listed, lev)).astype(jnp.int32)
        mine = jnp.broadcast_to(mine.astype(jnp.int32), (listed, lev)) > 0
        parts = []
        for begin in range(0, depth, lev):
            offset = wide + begin - start
            good = mine & (offset >= 0) & (offset < BLAT)
            picked = jnp.take_along_axis(table, jnp.clip(offset, 0, lev - 1), axis=1)
            parts.append(jnp.where(good, picked, 0.0))
        whole = jnp.concatenate(parts, axis=1)[:, :depth]
        high = whole.astype(jnp.bfloat16)
        low = (whole - high.astype(jnp.float32)).astype(jnp.bfloat16)
        sel[0:listed, :] = high
        sel[listed : 2 * listed, :] = low
        where = jnp.broadcast_to(table[:, BLAT + 1 : BLAT + 2], (listed, lev)).astype(
            jnp.int32
        ) + lax.rem(wide, BLEV)
        if not ready:
            load.wait()
            swap.wait_recv()
            halo_copy(0).wait_recv()
            ready = True

        for q in range(part):
            right = jnp.concatenate(
                [
                    jnp.concatenate(
                        [ext[0, q * group + g], ext[1, q * group + g], halo[q * group + g]], axis=0
                    )
                    for g in range(group)
                ],
                axis=1,
            )
            lifted = jnp.dot(sel[...], right, preferred_element_type=jnp.float32)
            lifted = lifted[:listed] + lifted[listed:]
            total = jnp.zeros((listed, lev), jnp.float32)
            for g in range(group):
                moved = jnp.take_along_axis(lifted[:, g * lev : (g + 1) * lev], where, axis=1)
                inside = (wide >= g * BLEV) & (wide < (g + 1) * BLEV)
                total = jnp.where(inside, moved, total)
            total = total.astype(jnp.bfloat16)
            for l in range(nlat):
                pieces[t, l, q] = total[l * slots : (l + 1) * slots]
            if (q + 1) % step == 0:
                for l in range(nlat):
                    if place_of == 2:
                        piece_copy(t, l, q // step, step).start()
                    else:
                        @pl.when((t != 1) | (lat != l))
                        def _():
                            piece_copy(t, l, q // step, step).start()

    keep = pltpu.make_async_copy(
        pieces.at[1, lat], recv.at[1, pair, pl.ds(side * part, part)], inc_sem
    )
    keep.start()
    jload.wait()
    keep.wait()
    span = width * BLEV
    level_row = (lax.broadcasted_iota(jnp.int32, (slots, lev), 1) // BLEV).astype(jnp.float32)
    which = lax.broadcasted_iota(jnp.int32, (slots, ntan), 0)
    answer = jnp.zeros((slots, ntan), jnp.float32)
    def begin_of(t):
        return t * span if isinstance(t, int) else pl.multiple_of(t * span, lev)

    def turn(k):
        for i in range(slots):
            turned[k, i // 2, :, pl.ds((i % 2) * ntan, ntan)] = jbuf[
                i, :, pl.ds(begin_of(collect[k + 1]), span)
            ].T

    def profile(t, low, high):
        flat = []
        for q in range(low, high):
            total = recv[t, 0, q].astype(jnp.float32)
            for p in range(1, npair):
                total = total + recv[t, p, q].astype(jnp.float32)
            at = level_row + jnp.asarray(t * width + q * group, jnp.int32).astype(jnp.float32)
            flat.append(jnp.where((at >= first) & (at <= last), total, 0.0))
        return jnp.concatenate(flat, axis=1).astype(jnp.bfloat16)

    for k, t in enumerate(collect):
        if k == 0:
            turn(1)
        if k == 2:
            for h in (1, 0):
                for l in range(h, nlat, 2):
                    piece_wait(t, l, 0, part)
                flat = profile(t, h * part, (h + 1) * part)
                for i in range(slots // 2):
                    both = jnp.dot(
                        flat, turned[1, i, h * (span // 2) : (h + 1) * (span // 2)],
                        preferred_element_type=jnp.float32,
                    )
                    answer = answer + jnp.where(which == 2 * i, both[:, :ntan], 0.0)
                    answer = answer + jnp.where(which == 2 * i + 1, both[:, ntan:], 0.0)
            break
        for l in others(t):
            piece_wait(t, l, 0, part)
        flat = profile(t, 0, nq)
        for i in range(slots // 2):
            if k == 0:
                block = jbuf[2 * i : 2 * i + 2, :, pl.ds(begin_of(t), span)].reshape(2 * ntan, span)
                both = lax.dot_general(
                    flat, block, (((1,), (1,)), ((), ())), preferred_element_type=jnp.float32
                )
            else:
                both = jnp.dot(flat, turned[k - 1, i], preferred_element_type=jnp.float32)
            answer = answer + jnp.where(which == 2 * i, both[:, :ntan], 0.0)
            answer = answer + jnp.where(which == 2 * i + 1, both[:, ntan:], 0.0)
        if k == 0:
            turn(0)
    out_ref[...] = answer

    swap.wait_send()

    @pl.when(side == 0)
    def _():
        halo_copy(0).wait_send()
        halo_copy(1).wait_send()

    @pl.when(lon > 0)
    def _():
        for l in others(0):
            info_copy(0, l).wait_send()

    @pl.when(relay_sector & (side == 1))
    def _():
        relay(0).wait_send()
        relay(1).wait_send()

    for t, l in every((2, 1)):
        info_copy(t, l).wait_send()
    for t, l in peers:
        piece_copy(t, l, 0, part).wait_send()


def local(nlon, nlat, increment, jacobian, lat_weight, centre, west, east, lat_offset, lev_offset):
    width, rows, lev = increment.shape
    slots, ntan, span = jacobian.shape
    nq = width * BLEV // lev
    vmem = pl.BlockSpec(memory_space=pltpu.VMEM)
    hbm = pl.BlockSpec(memory_space=pltpu.HBM)
    dma = pltpu.SemaphoreType.DMA
    ints = [v.reshape(1, slots) for v in (centre, west, east, lat_offset, lev_offset)]
    return pl.pallas_call(
        functools.partial(kernel, nlon, nlat),
        out_shape=pltpu.VMEM((slots, ntan), jnp.float32),
        in_specs=[hbm] * 8,
        out_specs=vmem,
        scratch_shapes=[
            pltpu.VMEM((BLAT, slots), jnp.float32),
            *[pltpu.VMEM((1, slots), jnp.int32)] * 5,
            dma((6,)),
            pltpu.VMEM((2, width // 2, rows, lev), jnp.bfloat16),
            pltpu.VMEM((width // 2, HALO, lev), jnp.bfloat16),
            pltpu.VMEM((slots, ntan, span), jnp.bfloat16),
            pltpu.VMEM((2, slots // 2, width * BLEV, 2 * ntan), jnp.bfloat16),
            pltpu.VMEM((3, nlat, slots * FIELDS // lev, lev), jnp.float32),
            pltpu.VMEM((2 * nlat * slots, 2 * rows + HALO), jnp.bfloat16),
            pltpu.VMEM((3, nlat, nq // 2, slots, lev), jnp.bfloat16),
            pltpu.VMEM((3, nlat // 2, nq, slots, lev), jnp.bfloat16),
            dma, dma, dma, dma, dma((2,)), dma,
            dma((3, nlat)), dma((3, nlat)), dma((2,)), dma, dma((3, nlat)), dma((3, nlat)),
        ],
        compiler_params=pltpu.CompilerParams(
            collective_id=0, has_side_effects=True, vmem_limit_bytes=56 << 20
        ),
    )(increment, jacobian, lat_weight.T, *ints)


def solution(mesh):
    return jax.shard_map(
        functools.partial(local, mesh.shape["lon"], mesh.shape["lat"]),
        mesh=mesh,
        in_specs=(
            P("lon", "lat", None),
            P(("lon", "lat"), None, None),
            P(("lon", "lat"), None),
            P(("lon", "lat")),
            P(("lon", "lat")),
            P(("lon", "lat")),
            P(("lon", "lat")),
            P(("lon", "lat")),
        ),
        out_specs=P(("lon", "lat"), None),
        check_vma=False,
    )
```

```python
import functools

import jax
import jax.numpy as jnp
from jax import lax
from jax.experimental import pallas as pl
from jax.experimental.pallas import tpu as pltpu
from jax.sharding import PartitionSpec as P

BLAT = 8
BLEV = 32
HALO = 8
FIELDS = 16
CHUNKS = 1
MESH = pl.DeviceIdType.MESH


def kernel(
    nlon, nlat, inc_ref, jac_ref, weight_hbm, centre_hbm, west_hbm, east_hbm, row_hbm, level_hbm,
    out_ref, weight_ref, centre_ref, west_ref, east_ref, row_ref, level_ref, small_sem,
    ext, halo, jbuf, turned, info, sel, pieces, recv,
    inc_sem, jac_sem, swap_send, swap_recv, halo_send, halo_recv,
    info_send, info_recv, pass_send, pass_recv, piece_send, piece_recv,
):
    lon = lax.axis_index("lon")
    lat = lax.axis_index("lat")
    width, rows, lev = inc_ref.shape
    slots, ntan = out_ref.shape
    group = lev // BLEV
    nq = width // group
    part = nq // 2
    half = width // 2
    listed = nlat * slots
    packed = lev // FIELDS
    pair = lat // 2
    side = lax.rem(lat, 2)
    npair = nlat // 2

    load = pltpu.make_async_copy(
        inc_ref.at[pl.ds(side * half, half)], ext.at[side], inc_sem
    )
    jload = pltpu.make_async_copy(jac_ref, jbuf, jac_sem)

    def sector(t):
        return lax.rem(lon + t - 1 + nlon, nlon)

    first_sector, relay_sector, last_sector = lon == 0, lon == 1, lon == nlon - 1
    odd = lax.rem(lon, 2)
    opening = first_sector.astype(jnp.int32)
    closing = last_sector.astype(jnp.int32)
    ahead = odd - closing
    later = odd + (lon == nlon - 2).astype(jnp.int32)
    relaying = relay_sector.astype(jnp.int32)
    serve = (1 - relaying, 2 - 2 * ahead + relaying, 2 * ahead)
    collect = (1, 2 - 2 * later, 2 * later)

    def others(t):
        own = isinstance(t, int) and t == 1
        return [lax.rem(lat + d, nlat) for d in range(1 if own else 0, nlat)]

    def every(chosen):
        return [(t, l) for t in chosen for l in others(t)]

    peers = []
    for t in (0, 2, 1):
        for d in range(nlat):
            if t != 1 or d:
                peers.append((t, lax.rem(lat + d, nlat)))

    barrier = pltpu.get_barrier_semaphore()

    def greet(t, l):
        pl.semaphore_signal(barrier, inc=1, device_id=(sector(t), l), device_id_type=MESH)

    @pl.when(last_sector)
    def _():
        pl.semaphore_signal(
            barrier, inc=1, device_id=(1, pair * 2 + 1), device_id_type=MESH
        )

    @pl.when(lon < nlon - 1)
    def _():
        for l in others(2):
            greet(2, l)

    for t, l in every((0, 1)):
        greet(t, l)
    small = [
        pltpu.make_async_copy(source, target, small_sem.at[i])
        for i, (source, target) in enumerate(
            [
                (weight_hbm, weight_ref), (row_hbm, row_ref), (level_hbm, level_ref),
                (centre_hbm, centre_ref), (west_hbm, west_ref), (east_hbm, east_ref),
            ]
        )
    ]
    for copy in small:
        copy.start()
    load.start()
    jload.start()

    eye = lax.broadcasted_iota(jnp.int32, (slots, slots), 0) == lax.broadcasted_iota(
        jnp.int32, (slots, slots), 1
    )

    def column(row):
        row = jnp.broadcast_to(row.astype(jnp.float32), (slots, slots))
        return jnp.sum(jnp.where(eye, row, 0.0), axis=1, keepdims=True)

    for copy in small:
        copy.wait()
    lane = lax.broadcasted_iota(jnp.int32, (slots, lev), 1)
    head = jnp.zeros((slots, lev), jnp.float32)
    for j in range(BLAT):
        head = jnp.where(lane == j, column(weight_ref[j : j + 1, :]), head)
    head = jnp.where(lane == BLAT, column(row_ref[...]), head)
    head = jnp.where(lane == BLAT + 1, column(level_ref[...]), head)
    place = lax.broadcasted_iota(jnp.int32, (slots, lev), 0)
    spread = jnp.take_along_axis(head, lax.rem(lane, FIELDS), axis=1)
    spread = jnp.where(lane // FIELDS == lax.rem(place, packed), spread, 0.0)
    info[1, lat] = jnp.concatenate(
        [
            jnp.sum(spread[r * packed : (r + 1) * packed], axis=0, keepdims=True)
            for r in range(slots // packed)
        ],
        axis=0,
    )
    middle = width + column(centre_ref[...])
    first = middle - column(west_ref[...])
    last = middle + column(east_ref[...])

    pl.semaphore_wait(
        barrier, len(peers) - nlat * opening + 2 * relaying * side
    )

    def info_copy(t, l):
        return pltpu.make_async_remote_copy(
            src_ref=info.at[1, lat], dst_ref=info.at[2 - t, lat],
            send_sem=info_send.at[t, l], recv_sem=info_recv.at[2 - t, lat],
            device_id=(sector(t), l), device_id_type=MESH,
        )

    def relay(other):
        return pltpu.make_async_remote_copy(
            src_ref=info.at[0], dst_ref=info.at[2],
            send_sem=pass_send.at[other], recv_sem=pass_recv,
            device_id=(nlon - 1, pair * 2 + other), device_id_type=MESH,
        )

    @pl.when(lon > 0)
    def _():
        for l in others(0):
            info_copy(0, l).start()

    for t, l in every((2, 1)):
        info_copy(t, l).start()
    swap = pltpu.make_async_remote_copy(
        src_ref=inc_ref.at[pl.ds((1 - side) * half, half)], dst_ref=ext.at[side],
        send_sem=swap_send, recv_sem=swap_recv,
        device_id=(lon, pair * 2 + 1 - side), device_id_type=MESH,
    )

    def halo_copy(other):
        return pltpu.make_async_remote_copy(
            src_ref=inc_ref.at[pl.ds(other * half, half), pl.ds(0, HALO), :], dst_ref=halo,
            send_sem=halo_send.at[other], recv_sem=halo_recv,
            device_id=(lon, lax.rem(pair + npair - 1, npair) * 2 + other), device_id_type=MESH,
        )

    @pl.when(side == 0)
    def _():
        halo_copy(0).start()
        halo_copy(1).start()

    swap.start()

    def info_wait(t, l):
        pltpu.make_async_remote_copy(
            src_ref=info.at[1, lat], dst_ref=info.at[t, l],
            send_sem=info_send.at[t, l], recv_sem=info_recv.at[t, l],
            device_id=(sector(t), l), device_id_type=MESH,
        ).wait_recv()

    @pl.when(relay_sector & (side == 1))
    def _():
        for l in others(0):
            info_wait(0, l)
        relay(0).start()
        relay(1).start()

    def slot(u, l, c, step):
        return recv.at[u, l // 2, pl.ds(lax.rem(l, 2) * part + c * step, step)]

    def piece_copy(t, l, c, step):
        return pltpu.make_async_remote_copy(
            src_ref=pieces.at[t, l, pl.ds(c * step, step)], dst_ref=slot(2 - t, lat, c, step),
            send_sem=piece_send.at[t, l], recv_sem=piece_recv.at[2 - t, lat],
            device_id=(sector(t), l), device_id_type=MESH,
        )

    def piece_wait(t, l, c, step):
        pltpu.make_async_remote_copy(
            src_ref=pieces.at[t, l, pl.ds(c * step, step)], dst_ref=slot(t, l, c, step),
            send_sem=piece_send.at[t, l], recv_sem=piece_recv.at[t, l],
            device_id=(sector(t), l), device_id_type=MESH,
        ).wait_recv()

    depth = 2 * rows + HALO
    wide = lax.broadcasted_iota(jnp.int32, (listed, lev), 1)
    unpack = lax.rem(
        lax.rem(lax.broadcasted_iota(jnp.int32, (listed, lev), 0), packed) * FIELDS + wide, lev
    )
    base = (pair * 2 * rows).astype(jnp.float32)

    ready = False
    step = part // CHUNKS
    for place_of, t in enumerate(serve):
        if place_of == 0:
            @pl.when(lon != 1)
            def _():
                for l in others(1):
                    info_wait(1, l)

            @pl.when(relay_sector & (side == 0))
            def _():
                for l in others(0):
                    info_wait(0, l)
        elif place_of == 1:
            @pl.when(last_sector)
            def _():
                relay(0).wait_recv()

            @pl.when(relay_sector)
            def _():
                for l in others(1):
                    info_wait(1, l)

            @pl.when((lon > 1) & (lon < nlon - 1) | first_sector)
            def _():
                for l in others(t):
                    info_wait(t, l)
        else:
            for l in others(t):
                info_wait(t, l)
        table = jnp.concatenate(
            [
                jnp.broadcast_to(info[t, l, r : r + 1, :], (packed, lev))
                for l in range(nlat)
                for r in range(slots // packed)
            ],
            axis=0,
        )
        table = jnp.take_along_axis(table, unpack, axis=1)
        local = table[:, BLAT : BLAT + 1] - base
        mine = (local >= 0.0) & (local < float(2 * rows))
        start = jnp.broadcast_to(local, (listed, lev)).astype(jnp.int32)
        mine = jnp.broadcast_to(mine.astype(jnp.int32), (listed, lev)) > 0
        parts = []
        for begin in range(0, depth, lev):
            offset = wide + begin - start
            good = mine & (offset >= 0) & (offset < BLAT)
            picked = jnp.take_along_axis(table, jnp.clip(offset, 0, lev - 1), axis=1)
            parts.append(jnp.where(good, picked, 0.0))
        whole = jnp.concatenate(parts, axis=1)[:, :depth]
        high = whole.astype(jnp.bfloat16)
        low = (whole - high.astype(jnp.float32)).astype(jnp.bfloat16)
        sel[0:listed, :] = high
        sel[listed : 2 * listed, :] = low
        where = jnp.broadcast_to(table[:, BLAT + 1 : BLAT + 2], (listed, lev)).astype(
            jnp.int32
        ) + lax.rem(wide, BLEV)
        if not ready:
            load.wait()
            swap.wait_recv()
            halo_copy(0).wait_recv()
            ready = True

        for q in range(part):
            right = jnp.concatenate(
                [
                    jnp.concatenate(
                        [ext[0, q * group + g], ext[1, q * group + g], halo[q * group + g]], axis=0
                    )
                    for g in range(group)
                ],
                axis=1,
            )
            lifted = jnp.dot(sel[...], right, preferred_element_type=jnp.float32)
            lifted = lifted[:listed] + lifted[listed:]
            total = jnp.zeros((listed, lev), jnp.float32)
            for g in range(group):
                moved = jnp.take_along_axis(lifted[:, g * lev : (g + 1) * lev], where, axis=1)
                inside = (wide >= g * BLEV) & (wide < (g + 1) * BLEV)
                total = jnp.where(inside, moved, total)
            total = total.astype(jnp.bfloat16)
            for l in range(nlat):
                pieces[t, l, q] = total[l * slots : (l + 1) * slots]
            if (q + 1) % step == 0:
                for l in range(nlat):
                    if place_of == 2:
                        piece_copy(t, l, q // step, step).start()
                    else:
                        @pl.when((t != 1) | (lat != l))
                        def _():
                            piece_copy(t, l, q // step, step).start()

    keep = pltpu.make_async_copy(
        pieces.at[1, lat], recv.at[1, pair, pl.ds(side * part, part)], inc_sem
    )
    keep.start()
    jload.wait()
    keep.wait()
    span = width * BLEV
    level_row = (lax.broadcasted_iota(jnp.int32, (slots, lev), 1) // BLEV).astype(jnp.float32)
    which = lax.broadcasted_iota(jnp.int32, (slots, ntan), 0)
    answer = jnp.zeros((slots, ntan), jnp.float32)
    def settle():
        swap.wait_send()

        @pl.when(side == 0)
        def _():
            halo_copy(0).wait_send()
            halo_copy(1).wait_send()

        @pl.when(lon > 0)
        def _():
            for l in others(0):
                info_copy(0, l).wait_send()

        @pl.when(relay_sector & (side == 1))
        def _():
            relay(0).wait_send()
            relay(1).wait_send()

        for t, l in every((2, 1)):
            info_copy(t, l).wait_send()
        for t, l in peers:
            piece_copy(t, l, 0, part).wait_send()

    def begin_of(t):
        return t * span if isinstance(t, int) else pl.multiple_of(t * span, lev)

    def turn(k):
        for i in range(slots):
            turned[k, i // 2, :, pl.ds((i % 2) * ntan, ntan)] = jbuf[
                i, :, pl.ds(begin_of(collect[k + 1]), span)
            ].T

    def profile(t, low, high):
        flat = []
        for q in range(low, high):
            total = recv[t, 0, q].astype(jnp.float32)
            for p in range(1, npair):
                total = total + recv[t, p, q].astype(jnp.float32)
            at = level_row + jnp.asarray(t * width + q * group, jnp.int32).astype(jnp.float32)
            flat.append(jnp.where((at >= first) & (at <= last), total, 0.0))
        return jnp.concatenate(flat, axis=1).astype(jnp.bfloat16)

    for k, t in enumerate(collect):
        if k == 0:
            turn(1)
        if k == 2:
            settle()
            for h in (1, 0):
                for l in range(h, nlat, 2):
                    piece_wait(t, l, 0, part)
                flat = profile(t, h * part, (h + 1) * part)
                for i in range(slots // 2):
                    both = jnp.dot(
                        flat, turned[1, i, h * (span // 2) : (h + 1) * (span // 2)],
                        preferred_element_type=jnp.float32,
                    )
                    answer = answer + jnp.where(which == 2 * i, both[:, :ntan], 0.0)
                    answer = answer + jnp.where(which == 2 * i + 1, both[:, ntan:], 0.0)
            break
        for l in others(t):
            piece_wait(t, l, 0, part)
        flat = profile(t, 0, nq)
        for i in range(slots // 2):
            if k == 0:
                block = jbuf[2 * i : 2 * i + 2, :, pl.ds(begin_of(t), span)].reshape(2 * ntan, span)
                both = lax.dot_general(
                    flat, block, (((1,), (1,)), ((), ())), preferred_element_type=jnp.float32
                )
            else:
                both = jnp.dot(flat, turned[k - 1, i], preferred_element_type=jnp.float32)
            answer = answer + jnp.where(which == 2 * i, both[:, :ntan], 0.0)
            answer = answer + jnp.where(which == 2 * i + 1, both[:, ntan:], 0.0)
        if k == 0:
            turn(0)
    out_ref[...] = answer


def local(nlon, nlat, increment, jacobian, lat_weight, centre, west, east, lat_offset, lev_offset):
    width, rows, lev = increment.shape
    slots, ntan, span = jacobian.shape
    nq = width * BLEV // lev
    vmem = pl.BlockSpec(memory_space=pltpu.VMEM)
    hbm = pl.BlockSpec(memory_space=pltpu.HBM)
    dma = pltpu.SemaphoreType.DMA
    ints = [v.reshape(1, slots) for v in (centre, west, east, lat_offset, lev_offset)]
    return pl.pallas_call(
        functools.partial(kernel, nlon, nlat),
        out_shape=pltpu.VMEM((slots, ntan), jnp.float32),
        in_specs=[hbm] * 8,
        out_specs=vmem,
        scratch_shapes=[
            pltpu.VMEM((BLAT, slots), jnp.float32),
            *[pltpu.VMEM((1, slots), jnp.int32)] * 5,
            dma((6,)),
            pltpu.VMEM((2, width // 2, rows, lev), jnp.bfloat16),
            pltpu.VMEM((width // 2, HALO, lev), jnp.bfloat16),
            pltpu.VMEM((slots, ntan, span), jnp.bfloat16),
            pltpu.VMEM((2, slots // 2, width * BLEV, 2 * ntan), jnp.bfloat16),
            pltpu.VMEM((3, nlat, slots * FIELDS // lev, lev), jnp.float32),
            pltpu.VMEM((2 * nlat * slots, 2 * rows + HALO), jnp.bfloat16),
            pltpu.VMEM((3, nlat, nq // 2, slots, lev), jnp.bfloat16),
            pltpu.VMEM((3, nlat // 2, nq, slots, lev), jnp.bfloat16),
            dma, dma, dma, dma, dma((2,)), dma,
            dma((3, nlat)), dma((3, nlat)), dma((2,)), dma, dma((3, nlat)), dma((3, nlat)),
        ],
        compiler_params=pltpu.CompilerParams(
            collective_id=0, has_side_effects=True, vmem_limit_bytes=56 << 20
        ),
    )(increment, jacobian, lat_weight.T, *ints)


def solution(mesh):
    return jax.shard_map(
        functools.partial(local, mesh.shape["lon"], mesh.shape["lat"]),
        mesh=mesh,
        in_specs=(
            P("lon", "lat", None),
            P(("lon", "lat"), None, None),
            P(("lon", "lat"), None),
            P(("lon", "lat")),
            P(("lon", "lat")),
            P(("lon", "lat")),
            P(("lon", "lat")),
            P(("lon", "lat")),
        ),
        out_specs=P(("lon", "lat"), None),
        check_vma=False,
    )
```

```python
import functools

import jax
import jax.numpy as jnp
from jax import lax
from jax.experimental import pallas as pl
from jax.experimental.pallas import tpu as pltpu
from jax.sharding import PartitionSpec as P

BLAT = 8
BLEV = 32
HALO = 8
FIELDS = 16
HALVES = (1, 2, 1)
MESH = pl.DeviceIdType.MESH


def kernel(
    nlon, nlat, inc_ref, jac_ref, weight_hbm, centre_hbm, west_hbm, east_hbm, row_hbm, level_hbm,
    out_ref, weight_ref, centre_ref, west_ref, east_ref, row_ref, level_ref, small_sem,
    ext, halo, jbuf, turned, info, sel, pieces, recv,
    inc_sem, jac_sem, swap_send, swap_recv, halo_send, halo_recv,
    info_send, info_recv, pass_send, pass_recv, piece_send, piece_recv,
):
    lon = lax.axis_index("lon")
    lat = lax.axis_index("lat")
    width, rows, lev = inc_ref.shape
    slots, ntan = out_ref.shape
    group = lev // BLEV
    nq = width // group
    part = nq // 2
    half = width // 2
    listed = nlat * slots
    packed = lev // FIELDS
    pair = lat // 2
    side = lax.rem(lat, 2)
    npair = nlat // 2

    load = pltpu.make_async_copy(
        inc_ref.at[pl.ds(side * half, half)], ext.at[side], inc_sem
    )
    jload = pltpu.make_async_copy(jac_ref, jbuf, jac_sem)

    def sector(t):
        return lax.rem(lon + t - 1 + nlon, nlon)

    first_sector, relay_sector, last_sector = lon == 0, lon == 1, lon == nlon - 1
    odd = lax.rem(lon, 2)
    opening = first_sector.astype(jnp.int32)
    closing = last_sector.astype(jnp.int32)
    ahead = odd - closing
    later = odd + (lon == nlon - 2).astype(jnp.int32)
    relaying = relay_sector.astype(jnp.int32)
    serve = (1 - relaying, 2 - 2 * ahead + relaying, 2 * ahead)
    collect = (1, 2 - 2 * later, 2 * later)

    def others(t):
        own = isinstance(t, int) and t == 1
        return [lax.rem(lat + d, nlat) for d in range(1 if own else 0, nlat)]

    def every(chosen):
        return [(t, l) for t in chosen for l in others(t)]

    peers = []
    for t in (0, 2, 1):
        for d in range(nlat):
            if t != 1 or d:
                peers.append((t, lax.rem(lat + d, nlat)))

    barrier = pltpu.get_barrier_semaphore()

    def greet(t, l):
        pl.semaphore_signal(barrier, inc=1, device_id=(sector(t), l), device_id_type=MESH)

    @pl.when(last_sector)
    def _():
        pl.semaphore_signal(
            barrier, inc=1, device_id=(1, pair * 2 + 1), device_id_type=MESH
        )

    @pl.when(lon < nlon - 1)
    def _():
        for l in others(2):
            greet(2, l)

    for t, l in every((0, 1)):
        greet(t, l)
    small = [
        pltpu.make_async_copy(source, target, small_sem.at[i])
        for i, (source, target) in enumerate(
            [
                (weight_hbm, weight_ref), (row_hbm, row_ref), (level_hbm, level_ref),
                (centre_hbm, centre_ref), (west_hbm, west_ref), (east_hbm, east_ref),
            ]
        )
    ]
    for copy in small:
        copy.start()
    load.start()
    jload.start()

    eye = lax.broadcasted_iota(jnp.int32, (slots, slots), 0) == lax.broadcasted_iota(
        jnp.int32, (slots, slots), 1
    )

    def column(row):
        row = jnp.broadcast_to(row.astype(jnp.float32), (slots, slots))
        return jnp.sum(jnp.where(eye, row, 0.0), axis=1, keepdims=True)

    for copy in small:
        copy.wait()
    lane = lax.broadcasted_iota(jnp.int32, (slots, lev), 1)
    head = jnp.zeros((slots, lev), jnp.float32)
    for j in range(BLAT):
        head = jnp.where(lane == j, column(weight_ref[j : j + 1, :]), head)
    head = jnp.where(lane == BLAT, column(row_ref[...]), head)
    head = jnp.where(lane == BLAT + 1, column(level_ref[...]), head)
    place = lax.broadcasted_iota(jnp.int32, (slots, lev), 0)
    spread = jnp.take_along_axis(head, lax.rem(lane, FIELDS), axis=1)
    spread = jnp.where(lane // FIELDS == lax.rem(place, packed), spread, 0.0)
    info[1, lat] = jnp.concatenate(
        [
            jnp.sum(spread[r * packed : (r + 1) * packed], axis=0, keepdims=True)
            for r in range(slots // packed)
        ],
        axis=0,
    )
    middle = width + column(centre_ref[...])
    first = middle - column(west_ref[...])
    last = middle + column(east_ref[...])

    pl.semaphore_wait(
        barrier, len(peers) - nlat * opening + 2 * relaying * side
    )

    def info_copy(t, l):
        return pltpu.make_async_remote_copy(
            src_ref=info.at[1, lat], dst_ref=info.at[2 - t, lat],
            send_sem=info_send.at[t, l], recv_sem=info_recv.at[2 - t, lat],
            device_id=(sector(t), l), device_id_type=MESH,
        )

    def relay(other):
        return pltpu.make_async_remote_copy(
            src_ref=info.at[0], dst_ref=info.at[2],
            send_sem=pass_send.at[other], recv_sem=pass_recv,
            device_id=(nlon - 1, pair * 2 + other), device_id_type=MESH,
        )

    @pl.when(lon > 0)
    def _():
        for l in others(0):
            info_copy(0, l).start()

    for t, l in every((2, 1)):
        info_copy(t, l).start()
    swap = pltpu.make_async_remote_copy(
        src_ref=inc_ref.at[pl.ds((1 - side) * half, half)], dst_ref=ext.at[side],
        send_sem=swap_send, recv_sem=swap_recv,
        device_id=(lon, pair * 2 + 1 - side), device_id_type=MESH,
    )

    def halo_copy(other):
        return pltpu.make_async_remote_copy(
            src_ref=inc_ref.at[pl.ds(other * half, half), pl.ds(0, HALO), :], dst_ref=halo,
            send_sem=halo_send.at[other], recv_sem=halo_recv,
            device_id=(lon, lax.rem(pair + npair - 1, npair) * 2 + other), device_id_type=MESH,
        )

    @pl.when(side == 0)
    def _():
        halo_copy(0).start()
        halo_copy(1).start()


    def info_wait(t, l):
        pltpu.make_async_remote_copy(
            src_ref=info.at[1, lat], dst_ref=info.at[t, l],
            send_sem=info_send.at[t, l], recv_sem=info_recv.at[t, l],
            device_id=(sector(t), l), device_id_type=MESH,
        ).wait_recv()

    @pl.when(relay_sector & (side == 1))
    def _():
        for l in others(0):
            info_wait(0, l)
        relay(0).start()
        relay(1).start()

    swap.start()

    def slot(u, l, c, step):
        return recv.at[u, l // 2, pl.ds(lax.rem(l, 2) * part + c * step, step)]

    def piece_copy(t, l, c, step):
        return pltpu.make_async_remote_copy(
            src_ref=pieces.at[t, l, pl.ds(c * step, step)], dst_ref=slot(2 - t, lat, c, step),
            send_sem=piece_send.at[t, l], recv_sem=piece_recv.at[2 - t, lat],
            device_id=(sector(t), l), device_id_type=MESH,
        )

    def piece_wait(t, l, c, step):
        pltpu.make_async_remote_copy(
            src_ref=pieces.at[t, l, pl.ds(c * step, step)], dst_ref=slot(t, l, c, step),
            send_sem=piece_send.at[t, l], recv_sem=piece_recv.at[t, l],
            device_id=(sector(t), l), device_id_type=MESH,
        ).wait_recv()

    depth = 2 * rows + HALO
    wide = lax.broadcasted_iota(jnp.int32, (listed, lev), 1)
    unpack = lax.rem(
        lax.rem(lax.broadcasted_iota(jnp.int32, (listed, lev), 0), packed) * FIELDS + wide, lev
    )
    base = (pair * 2 * rows).astype(jnp.float32)

    ready = False
    for place_of, t in enumerate(serve):
        halves = HALVES[place_of]
        count = listed // halves
        if place_of == 0:
            @pl.when(lon != 1)
            def _():
                for l in others(1):
                    info_wait(1, l)

            @pl.when(relay_sector & (side == 0))
            def _():
                for l in others(0):
                    info_wait(0, l)
        elif place_of == 1:
            @pl.when(last_sector)
            def _():
                relay(0).wait_recv()

            @pl.when(relay_sector)
            def _():
                for l in others(1):
                    info_wait(1, l)

            @pl.when((lon > 1) & (lon < nlon - 1) | first_sector)
            def _():
                for l in others(t):
                    info_wait(t, l)
        else:
            for l in others(t):
                info_wait(t, l)
        table = jnp.concatenate(
            [
                jnp.broadcast_to(info[t, l, r : r + 1, :], (packed, lev))
                for l in range(nlat)
                for r in range(slots // packed)
            ],
            axis=0,
        )
        table = jnp.take_along_axis(table, unpack, axis=1)
        local = table[:, BLAT : BLAT + 1] - base
        mine = (local >= 0.0) & (local < float(2 * rows))
        start = jnp.broadcast_to(local, (listed, lev)).astype(jnp.int32)
        mine = jnp.broadcast_to(mine.astype(jnp.int32), (listed, lev)) > 0
        parts = []
        for begin in range(0, depth, lev):
            offset = wide + begin - start
            good = mine & (offset >= 0) & (offset < BLAT)
            picked = jnp.take_along_axis(table, jnp.clip(offset, 0, lev - 1), axis=1)
            parts.append(jnp.where(good, picked, 0.0))
        whole = jnp.concatenate(parts, axis=1)[:, :depth]
        high = whole.astype(jnp.bfloat16)
        low = (whole - high.astype(jnp.float32)).astype(jnp.bfloat16)
        for h in range(halves):
            sel[2 * h * count : (2 * h + 1) * count, :] = high[h * count : (h + 1) * count]
            sel[(2 * h + 1) * count : (2 * h + 2) * count, :] = low[h * count : (h + 1) * count]
        where = jnp.broadcast_to(table[:, BLAT + 1 : BLAT + 2], (listed, lev)).astype(
            jnp.int32
        ) + lax.rem(wide, BLEV)
        if not ready:
            load.wait()
            swap.wait_recv()
            halo_copy(0).wait_recv()
            ready = True

        for h in range(halves):
            mine_where = where[h * count : (h + 1) * count]
            block_wide = wide[:count]
            targets = range(h * nlat // halves, (h + 1) * nlat // halves)
            for q in range(part):
                right = jnp.concatenate(
                    [
                        jnp.concatenate(
                            [ext[0, q * group + g], ext[1, q * group + g], halo[q * group + g]],
                            axis=0,
                        )
                        for g in range(group)
                    ],
                    axis=1,
                )
                lifted = jnp.dot(
                    sel[2 * h * count : (2 * h + 2) * count, :], right,
                    preferred_element_type=jnp.float32,
                )
                lifted = lifted[:count] + lifted[count:]
                total = jnp.zeros((count, lev), jnp.float32)
                for g in range(group):
                    moved = jnp.take_along_axis(
                        lifted[:, g * lev : (g + 1) * lev], mine_where, axis=1
                    )
                    inside = (block_wide >= g * BLEV) & (block_wide < (g + 1) * BLEV)
                    total = jnp.where(inside, moved, total)
                total = total.astype(jnp.bfloat16)
                for n, l in enumerate(targets):
                    pieces[t, l, q] = total[n * slots : (n + 1) * slots]
            for l in targets:
                if place_of == 2:
                    piece_copy(t, l, 0, part).start()
                else:
                    @pl.when((t != 1) | (lat != l))
                    def _():
                        piece_copy(t, l, 0, part).start()

    keep = pltpu.make_async_copy(
        pieces.at[1, lat], recv.at[1, pair, pl.ds(side * part, part)], inc_sem
    )
    keep.start()
    jload.wait()
    keep.wait()
    span = width * BLEV
    level_row = (lax.broadcasted_iota(jnp.int32, (slots, lev), 1) // BLEV).astype(jnp.float32)
    which = lax.broadcasted_iota(jnp.int32, (slots, ntan), 0)
    answer = jnp.zeros((slots, ntan), jnp.float32)
    def settle():
        swap.wait_send()

        @pl.when(side == 0)
        def _():
            halo_copy(0).wait_send()
            halo_copy(1).wait_send()

        @pl.when(lon > 0)
        def _():
            for l in others(0):
                info_copy(0, l).wait_send()

        @pl.when(relay_sector & (side == 1))
        def _():
            relay(0).wait_send()
            relay(1).wait_send()

        for t, l in every((2, 1)):
            info_copy(t, l).wait_send()
        for t, l in peers:
            piece_copy(t, l, 0, part).wait_send()

    def begin_of(t):
        return t * span if isinstance(t, int) else pl.multiple_of(t * span, lev)

    def turn(k):
        for i in range(slots):
            turned[k, i // 2, :, pl.ds((i % 2) * ntan, ntan)] = jbuf[
                i, :, pl.ds(begin_of(collect[k + 1]), span)
            ].T

    def profile(t, low, high):
        flat = []
        for q in range(low, high):
            total = recv[t, 0, q].astype(jnp.float32)
            for p in range(1, npair):
                total = total + recv[t, p, q].astype(jnp.float32)
            at = level_row + jnp.asarray(t * width + q * group, jnp.int32).astype(jnp.float32)
            flat.append(jnp.where((at >= first) & (at <= last), total, 0.0))
        return jnp.concatenate(flat, axis=1).astype(jnp.bfloat16)

    for k, t in enumerate(collect):
        if k == 0:
            turn(1)
        if k == 2:
            settle()
            for h in (1, 0):
                for l in range(h, nlat, 2):
                    piece_wait(t, l, 0, part)
                flat = profile(t, h * part, (h + 1) * part)
                for i in range(slots // 2):
                    both = jnp.dot(
                        flat, turned[1, i, h * (span // 2) : (h + 1) * (span // 2)],
                        preferred_element_type=jnp.float32,
                    )
                    answer = answer + jnp.where(which == 2 * i, both[:, :ntan], 0.0)
                    answer = answer + jnp.where(which == 2 * i + 1, both[:, ntan:], 0.0)
            break
        for l in others(t):
            piece_wait(t, l, 0, part)
        flat = profile(t, 0, nq)
        for i in range(slots // 2):
            if k == 0:
                block = jbuf[2 * i : 2 * i + 2, :, pl.ds(begin_of(t), span)].reshape(2 * ntan, span)
                both = lax.dot_general(
                    flat, block, (((1,), (1,)), ((), ())), preferred_element_type=jnp.float32
                )
            else:
                both = jnp.dot(flat, turned[k - 1, i], preferred_element_type=jnp.float32)
            answer = answer + jnp.where(which == 2 * i, both[:, :ntan], 0.0)
            answer = answer + jnp.where(which == 2 * i + 1, both[:, ntan:], 0.0)
        if k == 0:
            turn(0)
    out_ref[...] = answer


def local(nlon, nlat, increment, jacobian, lat_weight, centre, west, east, lat_offset, lev_offset):
    width, rows, lev = increment.shape
    slots, ntan, span = jacobian.shape
    nq = width * BLEV // lev
    vmem = pl.BlockSpec(memory_space=pltpu.VMEM)
    hbm = pl.BlockSpec(memory_space=pltpu.HBM)
    dma = pltpu.SemaphoreType.DMA
    ints = [v.reshape(1, slots) for v in (centre, west, east, lat_offset, lev_offset)]
    return pl.pallas_call(
        functools.partial(kernel, nlon, nlat),
        out_shape=pltpu.VMEM((slots, ntan), jnp.float32),
        in_specs=[hbm] * 8,
        out_specs=vmem,
        scratch_shapes=[
            pltpu.VMEM((BLAT, slots), jnp.float32),
            *[pltpu.VMEM((1, slots), jnp.int32)] * 5,
            dma((6,)),
            pltpu.VMEM((2, width // 2, rows, lev), jnp.bfloat16),
            pltpu.VMEM((width // 2, HALO, lev), jnp.bfloat16),
            pltpu.VMEM((slots, ntan, span), jnp.bfloat16),
            pltpu.VMEM((2, slots // 2, width * BLEV, 2 * ntan), jnp.bfloat16),
            pltpu.VMEM((3, nlat, slots * FIELDS // lev, lev), jnp.float32),
            pltpu.VMEM((2 * nlat * slots, 2 * rows + HALO), jnp.bfloat16),
            pltpu.VMEM((3, nlat, nq // 2, slots, lev), jnp.bfloat16),
            pltpu.VMEM((3, nlat // 2, nq, slots, lev), jnp.bfloat16),
            dma, dma, dma, dma, dma((2,)), dma,
            dma((3, nlat)), dma((3, nlat)), dma((2,)), dma, dma((3, nlat)), dma((3, nlat)),
        ],
        compiler_params=pltpu.CompilerParams(
            collective_id=0, has_side_effects=True, vmem_limit_bytes=56 << 20
        ),
    )(increment, jacobian, lat_weight.T, *ints)


def solution(mesh):
    return jax.shard_map(
        functools.partial(local, mesh.shape["lon"], mesh.shape["lat"]),
        mesh=mesh,
        in_specs=(
            P("lon", "lat", None),
            P(("lon", "lat"), None, None),
            P(("lon", "lat"), None),
            P(("lon", "lat")),
            P(("lon", "lat")),
            P(("lon", "lat")),
            P(("lon", "lat")),
            P(("lon", "lat")),
        ),
        out_specs=P(("lon", "lat"), None),
        check_vma=False,
    )
```

```python
import functools

import jax
import jax.numpy as jnp
from jax import lax
from jax.experimental import pallas as pl
from jax.experimental.pallas import tpu as pltpu
from jax.sharding import PartitionSpec as P

BLAT = 8
BLEV = 32
HALO = 8
FIELDS = 16
CHUNKS = 1
MESH = pl.DeviceIdType.MESH


def kernel(
    nlon, nlat, inc_ref, jac_ref, weight_hbm, centre_hbm, west_hbm, east_hbm, row_hbm, level_hbm,
    out_ref, weight_ref, centre_ref, west_ref, east_ref, row_ref, level_ref, small_sem,
    ext, halo, jbuf, turned, info, sel, pieces, recv,
    inc_sem, jac_sem, swap_send, swap_recv, halo_send, halo_recv,
    info_send, info_recv, pass_send, pass_recv, piece_send, piece_recv,
):
    lon = lax.axis_index("lon")
    lat = lax.axis_index("lat")
    width, rows, lev = inc_ref.shape
    slots, ntan = out_ref.shape
    group = lev // BLEV
    nq = width // group
    part = nq // 2
    half = width // 2
    listed = nlat * slots
    packed = lev // FIELDS
    pair = lat // 2
    side = lax.rem(lat, 2)
    npair = nlat // 2

    load = pltpu.make_async_copy(
        inc_ref.at[pl.ds(side * half, half)], ext.at[side], inc_sem
    )
    jload = pltpu.make_async_copy(jac_ref, jbuf, jac_sem)

    def sector(t):
        return lax.rem(lon + t - 1 + nlon, nlon)

    first_sector, relay_sector, last_sector = lon == 0, lon == 1, lon == nlon - 1
    odd = lax.rem(lon, 2)
    opening = first_sector.astype(jnp.int32)
    closing = last_sector.astype(jnp.int32)
    ahead = odd - closing
    later = odd + (lon == nlon - 2).astype(jnp.int32)
    relaying = relay_sector.astype(jnp.int32)
    serve = (1 - relaying, 2 - 2 * ahead + relaying, 2 * ahead)
    collect = (1, 2 - 2 * later, 2 * later)

    def others(t):
        own = isinstance(t, int) and t == 1
        return [lax.rem(lat + d, nlat) for d in range(1 if own else 0, nlat)]

    def every(chosen):
        return [(t, l) for t in chosen for l in others(t)]

    peers = []
    for t in (0, 2, 1):
        for d in range(nlat):
            if t != 1 or d:
                peers.append((t, lax.rem(lat + d, nlat)))

    barrier = pltpu.get_barrier_semaphore()

    def greet(t, l):
        pl.semaphore_signal(barrier, inc=1, device_id=(sector(t), l), device_id_type=MESH)

    @pl.when(last_sector)
    def _():
        pl.semaphore_signal(
            barrier, inc=1, device_id=(1, pair * 2 + 1), device_id_type=MESH
        )

    for t, l in every((0, 1)):
        greet(t, l)

    @pl.when(lon < nlon - 1)
    def _():
        for l in others(2):
            greet(2, l)

    small = [
        pltpu.make_async_copy(source, target, small_sem.at[i])
        for i, (source, target) in enumerate(
            [
                (weight_hbm, weight_ref), (row_hbm, row_ref), (level_hbm, level_ref),
                (centre_hbm, centre_ref), (west_hbm, west_ref), (east_hbm, east_ref),
            ]
        )
    ]
    for copy in small:
        copy.start()
    load.start()
    jload.start()

    eye = lax.broadcasted_iota(jnp.int32, (slots, slots), 0) == lax.broadcasted_iota(
        jnp.int32, (slots, slots), 1
    )

    def column(row):
        row = jnp.broadcast_to(row.astype(jnp.float32), (slots, slots))
        return jnp.sum(jnp.where(eye, row, 0.0), axis=1, keepdims=True)

    for copy in small:
        copy.wait()
    lane = lax.broadcasted_iota(jnp.int32, (slots, lev), 1)
    head = jnp.zeros((slots, lev), jnp.float32)
    for j in range(BLAT):
        head = jnp.where(lane == j, column(weight_ref[j : j + 1, :]), head)
    head = jnp.where(lane == BLAT, column(row_ref[...]), head)
    head = jnp.where(lane == BLAT + 1, column(level_ref[...]), head)
    place = lax.broadcasted_iota(jnp.int32, (slots, lev), 0)
    spread = jnp.take_along_axis(head, lax.rem(lane, FIELDS), axis=1)
    spread = jnp.where(lane // FIELDS == lax.rem(place, packed), spread, 0.0)
    info[1, lat] = jnp.concatenate(
        [
            jnp.sum(spread[r * packed : (r + 1) * packed], axis=0, keepdims=True)
            for r in range(slots // packed)
        ],
        axis=0,
    )
    middle = width + column(centre_ref[...])
    first = middle - column(west_ref[...])
    last = middle + column(east_ref[...])

    pl.semaphore_wait(
        barrier, len(peers) - nlat * opening + 2 * relaying * side
    )

    def info_copy(t, l):
        return pltpu.make_async_remote_copy(
            src_ref=info.at[1, lat], dst_ref=info.at[2 - t, lat],
            send_sem=info_send.at[t, l], recv_sem=info_recv.at[2 - t, lat],
            device_id=(sector(t), l), device_id_type=MESH,
        )

    def relay(other):
        return pltpu.make_async_remote_copy(
            src_ref=info.at[0], dst_ref=info.at[2],
            send_sem=pass_send.at[other], recv_sem=pass_recv,
            device_id=(nlon - 1, pair * 2 + other), device_id_type=MESH,
        )

    @pl.when(lon > 0)
    def _():
        for l in others(0):
            info_copy(0, l).start()

    for t, l in every((2, 1)):
        info_copy(t, l).start()
    swap = pltpu.make_async_remote_copy(
        src_ref=inc_ref.at[pl.ds((1 - side) * half, half)], dst_ref=ext.at[side],
        send_sem=swap_send, recv_sem=swap_recv,
        device_id=(lon, pair * 2 + 1 - side), device_id_type=MESH,
    )

    def halo_copy(other):
        return pltpu.make_async_remote_copy(
            src_ref=inc_ref.at[pl.ds(other * half, half), pl.ds(0, HALO), :], dst_ref=halo,
            send_sem=halo_send.at[other], recv_sem=halo_recv,
            device_id=(lon, lax.rem(pair + npair - 1, npair) * 2 + other), device_id_type=MESH,
        )

    @pl.when(side == 0)
    def _():
        halo_copy(0).start()
        halo_copy(1).start()

    swap.start()

    def info_wait(t, l):
        pltpu.make_async_remote_copy(
            src_ref=info.at[1, lat], dst_ref=info.at[t, l],
            send_sem=info_send.at[t, l], recv_sem=info_recv.at[t, l],
            device_id=(sector(t), l), device_id_type=MESH,
        ).wait_recv()

    @pl.when(relay_sector & (side == 1))
    def _():
        for l in others(0):
            info_wait(0, l)
        relay(0).start()
        relay(1).start()

    def slot(u, l, c, step):
        return recv.at[u, l // 2, pl.ds(lax.rem(l, 2) * part + c * step, step)]

    def piece_copy(t, l, c, step):
        return pltpu.make_async_remote_copy(
            src_ref=pieces.at[t, l, pl.ds(c * step, step)], dst_ref=slot(2 - t, lat, c, step),
            send_sem=piece_send.at[t, l], recv_sem=piece_recv.at[2 - t, lat],
            device_id=(sector(t), l), device_id_type=MESH,
        )

    def piece_wait(t, l, c, step):
        pltpu.make_async_remote_copy(
            src_ref=pieces.at[t, l, pl.ds(c * step, step)], dst_ref=slot(t, l, c, step),
            send_sem=piece_send.at[t, l], recv_sem=piece_recv.at[t, l],
            device_id=(sector(t), l), device_id_type=MESH,
        ).wait_recv()

    depth = 2 * rows + HALO
    wide = lax.broadcasted_iota(jnp.int32, (listed, lev), 1)
    unpack = lax.rem(
        lax.rem(lax.broadcasted_iota(jnp.int32, (listed, lev), 0), packed) * FIELDS + wide, lev
    )
    base = (pair * 2 * rows).astype(jnp.float32)

    ready = False
    step = part // CHUNKS
    for place_of, t in enumerate(serve):
        if place_of == 0:
            @pl.when(lon != 1)
            def _():
                for l in others(1):
                    info_wait(1, l)

            @pl.when(relay_sector & (side == 0))
            def _():
                for l in others(0):
                    info_wait(0, l)
        elif place_of == 1:
            @pl.when(last_sector)
            def _():
                relay(0).wait_recv()

            @pl.when(relay_sector)
            def _():
                for l in others(1):
                    info_wait(1, l)

            @pl.when((lon > 1) & (lon < nlon - 1) | first_sector)
            def _():
                for l in others(t):
                    info_wait(t, l)
        else:
            for l in others(t):
                info_wait(t, l)
        table = jnp.concatenate(
            [
                jnp.broadcast_to(info[t, l, r : r + 1, :], (packed, lev))
                for l in range(nlat)
                for r in range(slots // packed)
            ],
            axis=0,
        )
        table = jnp.take_along_axis(table, unpack, axis=1)
        local = table[:, BLAT : BLAT + 1] - base
        mine = (local >= 0.0) & (local < float(2 * rows))
        start = jnp.broadcast_to(local, (listed, lev)).astype(jnp.int32)
        mine = jnp.broadcast_to(mine.astype(jnp.int32), (listed, lev)) > 0
        parts = []
        for begin in range(0, depth, lev):
            offset = wide + begin - start
            good = mine & (offset >= 0) & (offset < BLAT)
            picked = jnp.take_along_axis(table, jnp.clip(offset, 0, lev - 1), axis=1)
            parts.append(jnp.where(good, picked, 0.0))
        whole = jnp.concatenate(parts, axis=1)[:, :depth]
        high = whole.astype(jnp.bfloat16)
        low = (whole - high.astype(jnp.float32)).astype(jnp.bfloat16)
        sel[0:listed, :] = high
        sel[listed : 2 * listed, :] = low
        where = jnp.broadcast_to(table[:, BLAT + 1 : BLAT + 2], (listed, lev)).astype(
            jnp.int32
        ) + lax.rem(wide, BLEV)
        if not ready:
            load.wait()
            swap.wait_recv()
            halo_copy(0).wait_recv()
            ready = True

        for q in range(part):
            right = jnp.concatenate(
                [
                    jnp.concatenate(
                        [ext[0, q * group + g], ext[1, q * group + g], halo[q * group + g]], axis=0
                    )
                    for g in range(group)
                ],
                axis=1,
            )
            lifted = jnp.dot(sel[...], right, preferred_element_type=jnp.float32)
            lifted = lifted[:listed] + lifted[listed:]
            total = jnp.zeros((listed, lev), jnp.float32)
            for g in range(group):
                moved = jnp.take_along_axis(lifted[:, g * lev : (g + 1) * lev], where, axis=1)
                inside = (wide >= g * BLEV) & (wide < (g + 1) * BLEV)
                total = jnp.where(inside, moved, total)
            total = total.astype(jnp.bfloat16)
            for l in range(nlat):
                pieces[t, l, q] = total[l * slots : (l + 1) * slots]
            if (q + 1) % step == 0:
                for l in range(nlat):
                    if place_of == 2:
                        piece_copy(t, l, q // step, step).start()
                    else:
                        @pl.when((t != 1) | (lat != l))
                        def _():
                            piece_copy(t, l, q // step, step).start()

    keep = pltpu.make_async_copy(
        pieces.at[1, lat], recv.at[1, pair, pl.ds(side * part, part)], inc_sem
    )
    keep.start()
    jload.wait()
    keep.wait()
    span = width * BLEV
    level_row = (lax.broadcasted_iota(jnp.int32, (slots, lev), 1) // BLEV).astype(jnp.float32)
    which = lax.broadcasted_iota(jnp.int32, (slots, ntan), 0)
    answer = jnp.zeros((slots, ntan), jnp.float32)
    def settle():
        swap.wait_send()

        @pl.when(side == 0)
        def _():
            halo_copy(0).wait_send()
            halo_copy(1).wait_send()

        @pl.when(lon > 0)
        def _():
            for l in others(0):
                info_copy(0, l).wait_send()

        @pl.when(relay_sector & (side == 1))
        def _():
            relay(0).wait_send()
            relay(1).wait_send()

        for t, l in every((2, 1)):
            info_copy(t, l).wait_send()
        for t, l in peers:
            piece_copy(t, l, 0, part).wait_send()

    def begin_of(t):
        return t * span if isinstance(t, int) else pl.multiple_of(t * span, lev)

    def turn(k):
        for i in range(slots):
            turned[k, i // 2, :, pl.ds((i % 2) * ntan, ntan)] = jbuf[
                i, :, pl.ds(begin_of(collect[k + 1]), span)
            ].T

    def profile(t, low, high):
        flat = []
        for q in range(low, high):
            total = recv[t, 0, q].astype(jnp.float32)
            for p in range(1, npair):
                total = total + recv[t, p, q].astype(jnp.float32)
            at = level_row + jnp.asarray(t * width + q * group, jnp.int32).astype(jnp.float32)
            flat.append(jnp.where((at >= first) & (at <= last), total, 0.0))
        return jnp.concatenate(flat, axis=1).astype(jnp.bfloat16)

    for k, t in enumerate(collect):
        if k == 0:
            turn(1)
        if k == 2:
            settle()
            for h in (1, 0):
                for l in range(h, nlat, 2):
                    piece_wait(t, l, 0, part)
                flat = profile(t, h * part, (h + 1) * part)
                for i in range(slots // 2):
                    both = jnp.dot(
                        flat, turned[1, i, h * (span // 2) : (h + 1) * (span // 2)],
                        preferred_element_type=jnp.float32,
                    )
                    answer = answer + jnp.where(which == 2 * i, both[:, :ntan], 0.0)
                    answer = answer + jnp.where(which == 2 * i + 1, both[:, ntan:], 0.0)
            break
        for l in others(t):
            piece_wait(t, l, 0, part)
        flat = profile(t, 0, nq)
        for i in range(slots // 2):
            if k == 0:
                block = jbuf[2 * i : 2 * i + 2, :, pl.ds(begin_of(t), span)].reshape(2 * ntan, span)
                both = lax.dot_general(
                    flat, block, (((1,), (1,)), ((), ())), preferred_element_type=jnp.float32
                )
            else:
                both = jnp.dot(flat, turned[k - 1, i], preferred_element_type=jnp.float32)
            answer = answer + jnp.where(which == 2 * i, both[:, :ntan], 0.0)
            answer = answer + jnp.where(which == 2 * i + 1, both[:, ntan:], 0.0)
        if k == 0:
            turn(0)
    out_ref[...] = answer


def local(nlon, nlat, increment, jacobian, lat_weight, centre, west, east, lat_offset, lev_offset):
    width, rows, lev = increment.shape
    slots, ntan, span = jacobian.shape
    nq = width * BLEV // lev
    vmem = pl.BlockSpec(memory_space=pltpu.VMEM)
    hbm = pl.BlockSpec(memory_space=pltpu.HBM)
    dma = pltpu.SemaphoreType.DMA
    ints = [v.reshape(1, slots) for v in (centre, west, east, lat_offset, lev_offset)]
    return pl.pallas_call(
        functools.partial(kernel, nlon, nlat),
        out_shape=pltpu.VMEM((slots, ntan), jnp.float32),
        in_specs=[hbm] * 8,
        out_specs=vmem,
        scratch_shapes=[
            pltpu.VMEM((BLAT, slots), jnp.float32),
            *[pltpu.VMEM((1, slots), jnp.int32)] * 5,
            dma((6,)),
            pltpu.VMEM((2, width // 2, rows, lev), jnp.bfloat16),
            pltpu.VMEM((width // 2, HALO, lev), jnp.bfloat16),
            pltpu.VMEM((slots, ntan, span), jnp.bfloat16),
            pltpu.VMEM((2, slots // 2, width * BLEV, 2 * ntan), jnp.bfloat16),
            pltpu.VMEM((3, nlat, slots * FIELDS // lev, lev), jnp.float32),
            pltpu.VMEM((2 * nlat * slots, 2 * rows + HALO), jnp.bfloat16),
            pltpu.VMEM((3, nlat, nq // 2, slots, lev), jnp.bfloat16),
            pltpu.VMEM((3, nlat // 2, nq, slots, lev), jnp.bfloat16),
            dma, dma, dma, dma, dma((2,)), dma,
            dma((3, nlat)), dma((3, nlat)), dma((2,)), dma, dma((3, nlat)), dma((3, nlat)),
        ],
        compiler_params=pltpu.CompilerParams(
            collective_id=0, has_side_effects=True, vmem_limit_bytes=56 << 20
        ),
    )(increment, jacobian, lat_weight.T, *ints)


def solution(mesh):
    return jax.shard_map(
        functools.partial(local, mesh.shape["lon"], mesh.shape["lat"]),
        mesh=mesh,
        in_specs=(
            P("lon", "lat", None),
            P(("lon", "lat"), None, None),
            P(("lon", "lat"), None),
            P(("lon", "lat")),
            P(("lon", "lat")),
            P(("lon", "lat")),
            P(("lon", "lat")),
            P(("lon", "lat")),
        ),
        out_specs=P(("lon", "lat"), None),
        check_vma=False,
    )
```
